256 devices in a mesh: blk: 32 (over z, y), view: 8 (over x, core).
Axes of the slice: x: 4, y: 4, z: 8, core: 2. Of those that a mesh axis runs over, the one named last changes fastest.
Arguments:
- estimate: float32 [512, 128, 256], P('blk'), may hold values from 0.3 to 3
- views: float32 [8, 512, 128, 256], P('view', 'blk'), may hold values from 0.3 to 3
- axial_taps: float32 [8, 33], P('view'), may hold values from 0.1 to 1
- lateral_taps: float32 [8, 2, 17], P('view'), may hold values from 0.05 to 1
- cover: int32 [8, 2], P('view'), may hold values from 0 to 512, as said below
Outputs:
- refined: float32 [512, 128, 256], P('blk')
The draws below stay inside these ranges and needn't reach their ends.
Inputs may be any that keep to these rules, and one draw needn't show every extreme that they name: cover[v, 0] < cover[v, 1]; every first plane is at most 128 and every end at least 384; some view starts at plane 0 and some view ends at 512.
All inputs are finite; a program needn't handle non-finite values.
Results may differ from the reference program's by a relative error of at most 0.00015.
Values sent between devices are 32-bit elements; how exact they have to be, the bound alone decides.
No kernel may reach another device: no remote copies, remote signals or barrier semaphores. Data moves between devices by JAX's collectives and lax.ppermute only.
A program may use at most 64 MiB of HBM per device.

```python
import math
import jax
import jax.numpy as jnp
from jax import lax

NY = 128
NX = 256
RAD = 8
RZ = 16
ITERS = 2
NZ = 512
VIEWS = 8
N_VIEW = 8


def draw_cover(key, part):
    first_key, second_key = jax.random.split(jax.random.fold_in(key, 17))
    starts = jax.random.randint(first_key, (N_VIEW,), 0, NZ // 4 + 1)
    starts = starts - jnp.min(starts)
    cuts = jax.random.randint(second_key, (N_VIEW,), 0, NZ // 4 + 1)
    ends = NZ - (cuts - jnp.min(cuts))
    return jnp.stack([starts, ends], axis=1).astype(jnp.int32)


def steps_of(rng, dims, pieces, smallest, high):
    factor_of = 1.0
    for dim, parts in pieces:
        heights = jax.random.uniform(jax.random.fold_in(jax.random.fold_in(rng, 6), dim), (parts,), jnp.float32, smallest / len(pieces), high / len(pieces))
        factor_of = factor_of * jnp.repeat(jnp.exp(heights), dims[dim] // parts).reshape((-1,) + (1,) * (len(dims) - 1 - dim))
    return factor_of


def setup_inputs(seed: int = 0) -> dict:
    streams_of = jax.random.split(jax.random.key(seed), 6)
    return {
        "estimate": jnp.clip(jnp.exp(math.log(3.0) - 2.3025851 * jax.random.uniform(streams_of[0], (NZ, NY, NX), jnp.float32) ** steps_of(streams_of[0], (NZ, NY, NX), ((0, 32),), -0.2, 0.2)), 0.3, 3.0),
        "views": jnp.clip(jnp.exp(math.log(3.0) - 2.3025851 * jax.random.uniform(streams_of[1], (VIEWS, NZ, NY, NX), jnp.float32) ** steps_of(streams_of[1], (VIEWS, NZ, NY, NX), ((0, 8), (1, 32)), -0.2, 0.2)), 0.3, 3.0),
        "axial_taps": jnp.clip(jnp.exp(math.log(1.0) - 2.3025851 * jax.random.uniform(streams_of[2], (VIEWS, 2 * RZ + 1), jnp.float32) ** steps_of(streams_of[2], (VIEWS, 2 * RZ + 1), ((0, 8),), -0.2, 0.2)), 0.1, 1.0),
        "lateral_taps": jnp.clip(jnp.exp(math.log(1.0) - 2.9957323 * jax.random.uniform(streams_of[3], (VIEWS, 2, 2 * RAD + 1), jnp.float32) ** steps_of(streams_of[3], (VIEWS, 2, 2 * RAD + 1), ((0, 8),), -0.2, 0.2)), 0.05, 1.0),
        "cover": draw_cover(jax.random.fold_in(streams_of[5], 71), 0),
    }


def blur_axis(field, taps, reach, axis):
    taps = taps / jnp.sum(taps)
    count = field.shape[axis]
    widths = [(0, 0)] * field.ndim
    widths[axis] = (reach, reach)
    padded = jnp.pad(field, widths)
    total = jnp.zeros_like(field)
    for offset in range(2 * reach + 1):
        piece = lax.slice_in_dim(padded, offset, offset + count, axis=axis)
        total = total + taps[offset] * piece
    return total


def reference(estimate, views, axial_taps, lateral_taps, cover):
    planes = jnp.arange(NZ)
    for step in range(ITERS):
        logsum = jnp.zeros_like(estimate)
        for v in range(VIEWS):
            blurred = blur_axis(estimate, lateral_taps[v, 1], RAD, 2)
            blurred = blur_axis(blurred, lateral_taps[v, 0], RAD, 1)
            blurred = blur_axis(blurred, axial_taps[v], RZ, 0)
            ratio = views[v] / blurred
            back = blur_axis(ratio, axial_taps[v][::-1], RZ, 0)
            back = blur_axis(back, lateral_taps[v, 1][::-1], RAD, 2)
            back = blur_axis(back, lateral_taps[v, 0][::-1], RAD, 1)
            inside = (planes >= cover[v, 0]) & (planes < cover[v, 1])
            logsum = logsum + jnp.where(inside[:, None, None], jnp.log(back), jnp.float32(0.0))
        estimate = estimate * jnp.exp(logsum)
    return estimate
```

```python
import functools

import jax
import jax.numpy as jnp
from jax import lax
from jax.experimental import pallas as pl
from jax.experimental.pallas import tpu as pltpu
from jax.sharding import PartitionSpec as P

RAD = 8
RZ = 16
ITERS = 2
YD = 4
XD = 4
F32 = jnp.float32
BF16 = jnp.bfloat16
NLAT = 2 * RAD + 1
NAX = 2 * RZ + 1

DIRS = ((-1, 0), (1, 0), (0, -1), (0, 1), (-1, -1), (-1, 1), (1, -1), (1, 1))
ANY = pl.BlockSpec(memory_space=pl.ANY)
SMEM = pl.BlockSpec(memory_space=pltpu.SMEM)
VMEM = pl.BlockSpec(memory_space=pltpu.VMEM)


def params():
    return pltpu.CompilerParams(vmem_limit_bytes=56 * 1024 * 1024)


def blk_shift(value, dz, dy):
    count = lax.axis_size("blk") // YD
    pairs = [
        (z * YD + y, (z + dz) * YD + y + dy)
        for z in range(count)
        for y in range(YD)
        if 0 <= z + dz < count and 0 <= y + dy < YD
    ]
    return lax.ppermute(value, "blk", pairs)


def y_turn(value, k):
    count = lax.axis_size("blk") // YD
    pairs = [(z * YD + y, z * YD + (y + k) % YD) for z in range(count) for y in range(YD)]
    return lax.ppermute(value, "blk", pairs)


def x_turn(value, k):
    pairs = [(2 * x + c, 2 * ((x + k) % XD) + c) for x in range(XD) for c in range(2)]
    return lax.ppermute(value, "view", pairs)


def core_swap(value):
    return lax.ppermute(value, "view", [(i, i ^ 1) for i in range(2 * XD)])


def split(value):
    high = value.astype(BF16)
    return high, (value - high.astype(F32)).astype(BF16)


def mm(a, b):
    return jnp.dot(a, b, preferred_element_type=F32)


def matrices_kernel(taps, kyh, kyl, kxh, kxl):
    row = lax.broadcasted_iota(jnp.int32, (128, 192), 0)
    col = lax.broadcasted_iota(jnp.int32, (128, 192), 1)
    one = jnp.int32(1)
    zero = jnp.int32(0)
    prow = sum(jnp.where(row >= 32 * n, one, zero) for n in (1, 2, 3))
    pcol = sum(jnp.where(col >= 48 * n, one, zero) for n in (1, 2, 3))
    near = jnp.where(prow == pcol, (col - 48 * pcol) - (row - 32 * prow), -1)
    wide = (
        lax.broadcasted_iota(jnp.int32, (256, 256), 0)
        - lax.broadcasted_iota(jnp.int32, (256, 256), 1)
        + RAD
    )
    for way in range(2):
        ky = jnp.zeros((128, 192), F32)
        kx = jnp.zeros((256, 256), F32)
        for d in range(NLAT):
            e = d if way == 0 else NLAT - 1 - d
            ky = jnp.where(near == d, taps[NAX + e], ky)
            kx = jnp.where(wide == d, taps[NAX + NLAT + e], kx)
        kyh[way], kyl[way] = split(ky)
        kxh[way], kxl[way] = split(kx)


def matrices(taps):
    ky = jax.ShapeDtypeStruct((2, 128, 192), BF16)
    kx = jax.ShapeDtypeStruct((2, 256, 256), BF16)
    return pl.pallas_call(
        matrices_kernel,
        out_shape=(ky, ky, kx, kx),
        in_specs=[SMEM],
        out_specs=(VMEM,) * 4,
        compiler_params=params(),
        name="matrices",
    )(taps)


def lateral(way, wide, kyh, kyl, kxh, kxl, across):
    @pl.loop(0, 24)
    def _(g):
        b = g // 4
        h = (g // 2) % 2
        s = g % 2
        block = wide[b, h, pl.ds(2 * s, 2)].reshape(192, 256)
        high, low = split(block)
        rows = mm(kyh[way], high) + (mm(kyl[way], high) + mm(kyh[way], low))
        high, low = split(rows)
        both = mm(high, kxh[way]) + (mm(low, kxh[way]) + mm(high, kxl[way]))
        across[pl.ds(4 * g, 4)] = both.reshape(4, 32, 256)


def axial(way, taps, across, finish):
    weights = [taps[d if way == 0 else NAX - 1 - d] for d in range(NAX)]

    @pl.loop(0, 16)
    def _(n):
        base = (n // 4) * 16
        rows = pl.ds(pl.multiple_of((n % 4) * 8, 8), 8)
        for half in range(2):
            lanes = pl.ds(half * 128, 128)
            sums = [None] * 16
            for j in range(48):
                value = across[base + j, rows, lanes]
                for o in range(max(0, j - 32), min(16, j + 1)):
                    term = weights[j - o] * value
                    sums[o] = term if sums[o] is None else sums[o] + term
            for o in range(16):
                finish(base + o, n // 4, o, rows, lanes, sums[o])


def halo_slot(wide, direction, halves):
    dz, dy = direction
    b = {1: 0, -1: 5, 0: pl.ds(1, 4)}[dz]
    r = {1: pl.ds(0, 8), -1: pl.ds(40, 8), 0: pl.ds(8, 32)}[dy]
    return wide.at[b, halves, :, :, r, :]


def edge_of(tile, direction):
    dz, dy = direction
    b = {-1: 0, 1: 3, 0: pl.ds(0, 4)}[dz]
    r = {-1: pl.ds(0, 8), 1: pl.ds(24, 8), 0: pl.ds(0, 32)}[dy]
    if len(tile.shape) == 6:
        return tile.at[b, :, :, :, r, :]
    return tile.at[b, :, :, r, :]


def place():
    blk = lax.axis_index("blk")
    view = lax.axis_index("view")
    return blk // YD, blk % YD, view // 2, view % 2


def run(copies):
    for copy in copies:
        copy.start()
    return copies


def forward_kernel(taps, kyh, kyl, kxh, kxl, *refs):
    pieces, halos, shown = refs[:8], refs[8:24], refs[24:28]
    center, edges = refs[28], refs[29:37]
    wide, across, views, ratio, sems = refs[37:]
    z, y, x, c = place()
    copies = []

    def copy(source, target):
        copies.append(pltpu.make_async_copy(source, target, sems.at[len(copies)]))

    for k in range(4):
        s = (x - k + XD) % XD
        for other in range(2):
            half = c if other == 0 else 1 - c
            copy(pieces[4 * other + k], wide.at[pl.ds(1, 4), half, s, :, pl.ds(8, 32), :])
    for n, direction in enumerate(DIRS):
        for other in range(2):
            half = c if other == 0 else 1 - c
            copy(halos[8 * other + n], halo_slot(wide, direction, half))
    for k in range(4):
        b = (y - k + YD) % YD
        copy(shown[k], views.at[pl.ds(pl.multiple_of(16 * b, 16), 16)])
    run(copies)
    for item in copies[:24]:
        item.wait()
    lateral(0, wide, kyh, kyl, kxh, kxl, across)
    for item in copies[24:]:
        item.wait()

    def finish(plane, b, o, rows, lanes, value):
        ratio[b, o // 8, (o % 8) // 2, o % 2, rows, lanes] = views[plane, rows, lanes] / value

    axial(0, taps, across, finish)
    del copies[:]
    copy(ratio, center)
    for n, direction in enumerate(DIRS):
        copy(edge_of(ratio, direction), edges[n])
    for item in run(copies):
        item.wait()


def edge_shape(direction, lead):
    dz, dy = direction
    return ((4,) if dz == 0 else ()) + lead + (4, 2, 32 if dy == 0 else 8, 256)


def forward(taps, mats, pieces, halos, shown):
    outs = [jax.ShapeDtypeStruct((4, 2, 4, 2, 32, 256), F32)]
    outs += [jax.ShapeDtypeStruct(edge_shape(d, (2,)), F32) for d in DIRS]
    got = pl.pallas_call(
        forward_kernel,
        out_shape=tuple(outs),
        in_specs=[SMEM] + [VMEM] * 4 + [ANY] * 28,
        out_specs=(ANY,) * 9,
        scratch_shapes=[
            pltpu.VMEM((6, 2, 4, 2, 48, 256), F32),
            pltpu.VMEM((96, 32, 256), F32),
            pltpu.VMEM((64, 32, 256), F32),
            pltpu.VMEM((4, 2, 4, 2, 32, 256), F32),
            pltpu.SemaphoreType.DMA((28,)),
        ],
        compiler_params=params(),
        name="forward",
    )(taps, *mats, *pieces, *halos, *shown)
    return got[0], got[1:]


def backward_kernel(taps, cover, kyh, kyl, kxh, kxl, *refs):
    center, halos = refs[0], refs[1:9]
    mine, other = refs[9:11]
    wide, across, logs, sems = refs[11:]
    z, y, x, c = place()
    copies = []

    def copy(source, target):
        copies.append(pltpu.make_async_copy(source, target, sems.at[len(copies)]))

    both = pl.ds(0, 2)
    copy(center, wide.at[pl.ds(1, 4), :, :, :, pl.ds(8, 32), :])
    for n, direction in enumerate(DIRS):
        copy(halos[n], halo_slot(wide, direction, both))
    for item in run(copies):
        item.wait()
    lateral(1, wide, kyh, kyl, kxh, kxl, across)
    first = cover[0]
    end = cover[1]

    def finish(plane, b, o, rows, lanes, value):
        at = z * 64 + plane
        inside = jnp.logical_and(at >= first, at < end)
        logs[b, o // 8, (o % 8) // 2, o % 2, rows, lanes] = jnp.where(
            inside, jnp.log(value), jnp.float32(0.0)
        )

    axial(1, taps, across, finish)
    del copies[:]
    copy(logs.at[:, c], mine)
    copy(logs.at[:, 1 - c], other)
    for item in run(copies):
        item.wait()


def backward(taps, cover, mats, center, halos):
    half = jax.ShapeDtypeStruct((4, 4, 2, 32, 256), F32)
    return pl.pallas_call(
        backward_kernel,
        out_shape=(half, half),
        in_specs=[SMEM, SMEM] + [VMEM] * 4 + [ANY] * 9,
        out_specs=(ANY, ANY),
        scratch_shapes=[
            pltpu.VMEM((6, 2, 4, 2, 48, 256), F32),
            pltpu.VMEM((96, 32, 256), F32),
            pltpu.VMEM((4, 2, 4, 2, 32, 256), F32),
            pltpu.SemaphoreType.DMA((9,)),
        ],
        compiler_params=params(),
        name="backward",
    )(taps, cover, *mats, center, *halos)


def shares_kernel(mine, got, *outs):
    z, y, x, c = place()
    for k in range(4):
        s = (x + k) % XD
        outs[k][...] = mine[:, s] + got[:, s]


def shares(mine, got):
    part = jax.ShapeDtypeStruct((4, 2, 32, 256), F32)
    return pl.pallas_call(
        shares_kernel,
        out_shape=(part,) * 4,
        in_specs=[VMEM, VMEM],
        out_specs=(VMEM,) * 4,
        compiler_params=params(),
        name="shares",
    )(mine, got)


def edges_kernel(*refs):
    pieces, outs = refs[:4], refs[4:12]
    tile, sems = refs[12:]
    z, y, x, c = place()
    copies = []

    def copy(source, target):
        copies.append(pltpu.make_async_copy(source, target, sems.at[len(copies)]))

    for k in range(4):
        copy(pieces[k], tile.at[:, (x - k + XD) % XD])
    for item in run(copies):
        item.wait()
    del copies[:]
    for n, direction in enumerate(DIRS):
        copy(edge_of(tile, direction), outs[n])
    for item in run(copies):
        item.wait()


def edges(pieces):
    return pl.pallas_call(
        edges_kernel,
        out_shape=tuple(jax.ShapeDtypeStruct(edge_shape(d, ()), F32) for d in DIRS),
        in_specs=[ANY] * 4,
        out_specs=(ANY,) * 8,
        scratch_shapes=[
            pltpu.VMEM((4, 4, 2, 32, 256), F32),
            pltpu.SemaphoreType.DMA((8,)),
        ],
        compiler_params=params(),
        name="edges",
    )(*pieces)


def slab_kernel(*refs):
    pieces, out = refs[:8], refs[8]
    slab, sems = refs[9:]
    z, y, x, c = place()
    copies = []

    def copy(source, target):
        copies.append(pltpu.make_async_copy(source, target, sems.at[len(copies)]))

    for k in range(4):
        s = (x - k + XD) % XD
        for other in range(2):
            half = c if other == 0 else 1 - c
            copy(pieces[4 * other + k], slab.at[half, s])
    for item in run(copies):
        item.wait()
    del copies[:]
    copy(slab, out)
    for item in run(copies):
        item.wait()


def slab(pieces):
    return pl.pallas_call(
        slab_kernel,
        out_shape=jax.ShapeDtypeStruct((2, 4, 2, 128, 256), F32),
        in_specs=[ANY] * 8,
        out_specs=ANY,
        scratch_shapes=[
            pltpu.VMEM((2, 4, 2, 128, 256), F32),
            pltpu.SemaphoreType.DMA((8,)),
        ],
        compiler_params=params(),
        name="slab",
    )(*pieces)


def by_block(pieces, y):
    order = [pieces[0], pieces[3], pieces[2], pieces[1]]
    stack = jnp.stack(order + order[:3])
    return lax.dynamic_slice_in_dim(stack, (YD - y) % YD, 4, axis=0)


def gathered(share):
    return [share] + [x_turn(share, k) for k in (1, 2, 3)]


def local(estimate, views, axial_taps, lateral_taps, cover):
    z, y, x, c = place()
    taps = jnp.concatenate(
        [
            axial_taps[0] / jnp.sum(axial_taps[0]),
            lateral_taps[0, 0] / jnp.sum(lateral_taps[0, 0]),
            lateral_taps[0, 1] / jnp.sum(lateral_taps[0, 1]),
        ]
    )
    mats = matrices(taps)
    cover = cover[0]

    def rows_for(value, k, axis):
        return lax.dynamic_slice_in_dim(value, 32 * ((y + k) % YD), 32, axis=axis)

    own = lax.dynamic_slice_in_dim(estimate, 8 * c + 2 * x, 2, axis=0)
    parts = [rows_for(own, 0, 1)] + [y_turn(rows_for(own, k, 1), k) for k in (1, 2, 3)]
    share = by_block(parts, y)
    shown = [rows_for(views[0], 0, 1)]
    shown += [y_turn(rows_for(views[0], k, 1), k) for k in (1, 2, 3)]
    for step in range(ITERS):
        pieces = gathered(share)
        swapped = [core_swap(piece) for piece in pieces]
        halos = [blk_shift(e, *d) for e, d in zip(edges(pieces), DIRS)]
        halos += [core_swap(halo) for halo in halos]
        center, rims = forward(taps, mats, pieces + swapped, halos, shown)
        halos = [blk_shift(e, *d) for e, d in zip(rims, DIRS)]
        mine, other = backward(taps, cover, mats, center, halos)
        terms = shares(mine, core_swap(other))
        total = terms[0]
        for k in (1, 2, 3):
            total = total + x_turn(terms[k], k)
        share = share * jnp.exp(total)
    parts = [lax.dynamic_index_in_dim(share, (y + k) % YD, 0, keepdims=False) for k in range(4)]
    parts = [parts[0]] + [y_turn(parts[k], k) for k in (1, 2, 3)]
    strip = by_block(parts, y)
    strip = jnp.transpose(strip, (1, 0, 2, 3)).reshape(2, 128, 256)
    pieces = gathered(strip)
    pieces = pieces + [core_swap(piece) for piece in pieces]
    return slab(pieces).reshape(16, 128, 256)


def solution(mesh):
    in_specs = (
        P("blk", None, None),
        P("view", "blk", None, None),
        P("view", None),
        P("view", None, None),
        P("view", None),
    )
    out_specs = P("blk", None, None)
    return jax.shard_map(local, mesh=mesh, in_specs=in_specs, out_specs=out_specs, check_vma=False)
```

```python
import jax
import jax.numpy as jnp
from jax import lax
from jax.experimental import pallas as pl
from jax.experimental.pallas import tpu as pltpu
from jax.sharding import PartitionSpec as P

RAD = 8
RZ = 16
ITERS = 2
YD = 4
XD = 4
F32 = jnp.float32
BF16 = jnp.bfloat16
NLAT = 2 * RAD + 1
NAX = 2 * RZ + 1

ANY = pl.BlockSpec(memory_space=pl.ANY)
SMEM = pl.BlockSpec(memory_space=pltpu.SMEM)
VMEM = pl.BlockSpec(memory_space=pltpu.VMEM)
STEPS = (((1, 0), (0, 1)), ((-1, 0), (0, -1)), ((1, 1), (1, -1)), ((-1, -1), (-1, 1)))


def params():
    return pltpu.CompilerParams(vmem_limit_bytes=56 * 1024 * 1024)


def blk_shift(value, dz, dy):
    count = lax.axis_size("blk") // YD
    pairs = [
        (z * YD + y, (z + dz) * YD + y + dy)
        for z in range(count)
        for y in range(YD)
        if 0 <= z + dz < count and 0 <= y + dy < YD
    ]
    return lax.ppermute(value, "blk", pairs)


def core_step(value, steps):
    count = lax.axis_size("blk") // YD
    views = lax.axis_size("view")
    pairs = []
    for z in range(count):
        for y in range(YD):
            for v in range(views):
                dz, dy = steps[v % 2]
                if 0 <= z + dz < count and 0 <= y + dy < YD:
                    target = (z + dz) * YD + y + dy
                    pairs.append(((z * YD + y) * views + v, target * views + v))
    return lax.ppermute(value, ("blk", "view"), pairs)


def y_turn(value, k):
    count = lax.axis_size("blk") // YD
    pairs = [(z * YD + y, z * YD + (y + k) % YD) for z in range(count) for y in range(YD)]
    return lax.ppermute(value, "blk", pairs)


def x_turn(value, k):
    pairs = [(2 * x + c, 2 * ((x + k) % XD) + c) for x in range(XD) for c in range(2)]
    return lax.ppermute(value, "view", pairs)


def core_swap(value):
    return lax.ppermute(value, "view", [(i, i ^ 1) for i in range(2 * XD)])


def split(value):
    high = value.astype(BF16)
    return high, (value - high.astype(F32)).astype(BF16)


def mm(a, b):
    return jnp.dot(a, b, preferred_element_type=F32)


def matrices_kernel(axial_taps, lateral_taps, kyh, kyl, kxh, kxl, kzh, kzl):
    row = lax.broadcasted_iota(jnp.int32, (128, 192), 0)
    col = lax.broadcasted_iota(jnp.int32, (128, 192), 1)
    one = jnp.int32(1)
    zero = jnp.int32(0)
    prow = sum(jnp.where(row >= 32 * n, one, zero) for n in (1, 2, 3))
    pcol = sum(jnp.where(col >= 48 * n, one, zero) for n in (1, 2, 3))
    near = jnp.where(prow == pcol, (col - 48 * pcol) - (row - 32 * prow), -1)

    def offset(shape, sign, shift):
        return shift + sign * (
            lax.broadcasted_iota(jnp.int32, shape, 0) - lax.broadcasted_iota(jnp.int32, shape, 1)
        )

    wide = offset((256, 256), 1, RAD)
    deep = offset((64, 96), -1, 0)

    def total(tap, count):
        return lax.fori_loop(0, count, lambda d, acc: acc + tap(d), jnp.float32(0.0))

    def fill(where, tap, count, high, low):
        norm = total(tap, count)
        for way in range(2):

            def put(d, acc, way=way):
                return jnp.where(where == d, tap(d if way == 0 else count - 1 - d), acc)

            matrix = lax.fori_loop(0, count, put, jnp.zeros(where.shape, F32))
            high[way], low[way] = split(matrix / jnp.full(where.shape, norm))

    fill(near, lambda d: lateral_taps[0, 0, d], NLAT, kyh, kyl)
    fill(wide, lambda d: lateral_taps[0, 1, d], NLAT, kxh, kxl)
    fill(deep, lambda d: axial_taps[0, d], NAX, kzh, kzl)


def matrices(axial_taps, lateral_taps):
    ky = jax.ShapeDtypeStruct((2, 128, 192), BF16)
    kx = jax.ShapeDtypeStruct((2, 256, 256), BF16)
    kz = jax.ShapeDtypeStruct((2, 64, 96), BF16)
    return pl.pallas_call(
        matrices_kernel,
        out_shape=(ky, ky, kx, kx, kz, kz),
        in_specs=[SMEM, SMEM],
        out_specs=(VMEM,) * 6,
        compiler_params=params(),
        name="matrices",
    )(axial_taps, lateral_taps)


def both_halves(ref, group, rows):
    return jnp.concatenate([ref[0, group, rows, :], ref[1, group, rows, :]], axis=1)


def store_halves(ref, group, rows, value):
    ref[0, group, rows, :] = value[:, :128]
    ref[1, group, rows, :] = value[:, 128:]


def blur(way, mats, wide, across, finish):
    kyh, kyl, kxh, kxl, kzh, kzl = [m[way] for m in mats]

    @pl.loop(0, 6)
    def _(b):
        for n in range(4):
            block = wide[b, n // 2, pl.ds(2 * (n % 2), 2)].reshape(192, 256)
            high, low = split(block)
            rows = mm(kyh, high) + (mm(kyl, high) + mm(kyh, low))
            for p in range(4):
                at = pl.ds(pl.multiple_of(128 * b + 32 * n + 8 * p, 8), 8)
                for q in range(4):
                    store_halves(across, q, at, rows[32 * p + 8 * q : 32 * p + 8 * q + 8])

    @pl.loop(0, 8)
    def _(n):
        deep = []
        for r in range(4):
            high, low = split(both_halves(across, n // 2, pl.ds(4 * (n % 2) + r, 96, stride=8)))
            deep.append(mm(kzh, high) + (mm(kzl, high) + mm(kzh, low)))
        high, low = split(jnp.concatenate(deep, axis=0))
        both = mm(high, kxh) + (mm(low, kxh) + mm(high, kxl))
        for r in range(4):
            rows = pl.ds(4 * (n % 2) + r, 64, stride=8)
            finish(n // 2, rows, both[64 * r : 64 * r + 64])


def halo_slot(wide, step):
    dz, dy = step
    b = {1: 0, -1: 5, 0: pl.ds(1, 4)}[dz]
    r = {1: 0, -1: 5, 0: pl.ds(1, 4)}[dy]
    return wide.at[b, :, :, :, r]


def edge_of(tile, step):
    dz, dy = step
    b = {-1: 0, 1: 3, 0: pl.ds(0, 4)}[dz]
    r = {-1: 0, 1: 3, 0: pl.ds(0, 4)}[dy]
    return tile.at[b, :, :, :, r]


def place():
    blk = lax.axis_index("blk")
    view = lax.axis_index("view")
    return blk // YD, blk % YD, view // 2, view % 2


class Copies:
    def __init__(self, sems):
        self.sems = sems
        self.items = []

    def add(self, source, target):
        item = pltpu.make_async_copy(source, target, self.sems.at[len(self.items)])
        item.start()
        self.items.append(item)

    def add_by_core(self, c, pair0, pair1):
        items = [pltpu.make_async_copy(*p, self.sems.at[len(self.items)]) for p in (pair0, pair1)]
        pl.when(c == 0)(items[0].start)
        pl.when(c != 0)(items[1].start)
        self.items.append(items[0])

    def wait(self, first=0, end=None):
        for item in self.items[first:end]:
            item.wait()


TILE = (4, 2, 4, 2, 4, 8, 256)
WIDE = (6, 2, 4, 2, 6, 8, 256)
ZEDGE = (2, 4, 2, 4, 8, 256)
YEDGE = (4, 2, 4, 2, 8, 256)
CORNER = (2, 4, 2, 8, 256)
PART = (4, 2, 4, 8, 256)
RATIO = (4, 4, 2, 4, 2, 8, 256)
RATIO_ZEDGE = (4, 2, 4, 2, 8, 256)
FACES = ((1, 0), (-1, 0), (0, 1), (0, -1))


def grouped(ref, half):
    return ref.at[half].reshape(4, 4, 2, 4, 2, 8, 128)


def put_pieces(copies, pieces, tile, x, c):
    for k in range(4):
        s = (x - k + XD) % XD
        for other in range(2):
            half = c if other == 0 else 1 - c
            copies.add(pieces[4 * other + k], tile(half, s))


def forward_kernel(*refs):
    mats, pieces, halos, shown = refs[:6], refs[6:14], refs[14:26], refs[26:30]
    center, edges = refs[30], refs[31:35]
    wide, across, views, ratio, sems, out_sems = refs[35:]
    z, y, x, c = place()
    copies = Copies(sems)
    put_pieces(copies, pieces, lambda h, s: wide.at[pl.ds(1, 4), h, s, :, pl.ds(1, 4)], x, c)
    for n, steps in enumerate(STEPS):
        if n < 2:
            own, got = halos[4 * n : 4 * n + 2], halos[4 * n + 2 : 4 * n + 4]
        else:
            own, got = (halos[4 + 2 * n],) * 2, (halos[5 + 2 * n],) * 2
        slots = [halo_slot(wide, step) for step in steps]
        copies.add_by_core(c, (own[0], slots[0]), (got[0], slots[0]))
        copies.add_by_core(c, (got[1], slots[1]), (own[1], slots[1]))
    for k in range(4):
        b = (y - k + YD) % YD
        for half in range(2):
            copies.add(shown[k].at[..., pl.ds(128 * half, 128)], grouped(views, half).at[:, b])
    copies.wait()

    def finish(group, rows, value):
        store_halves(ratio, group, rows, both_halves(views, group, rows) / value)

    blur(0, mats, wide, across, finish)
    copies = Copies(out_sems)
    for half in range(2):
        tile = grouped(ratio, half)
        lanes = pl.ds(128 * half, 128)
        for n, edge in enumerate((tile.at[:, 3], tile.at[:, 0], tile.at[3], tile.at[0])):
            copies.add(edge, edges[n].at[..., lanes])
        copies.add(tile, center.at[..., lanes])
    copies.wait()


def forward(mats, pieces, halos, shown):
    shapes = (RATIO, RATIO_ZEDGE, RATIO_ZEDGE, YEDGE, YEDGE)
    got = pl.pallas_call(
        forward_kernel,
        out_shape=tuple(jax.ShapeDtypeStruct(s, F32) for s in shapes),
        in_specs=[VMEM] * 6 + [ANY] * 24,
        out_specs=(ANY,) * 5,
        scratch_shapes=[
            pltpu.VMEM(WIDE, F32),
            pltpu.VMEM((2, 4, 768, 128), F32),
            pltpu.VMEM((2, 4, 512, 128), F32),
            pltpu.VMEM((2, 4, 512, 128), F32),
            pltpu.SemaphoreType.DMA((24,)),
            pltpu.SemaphoreType.DMA((10,)),
        ],
        compiler_params=params(),
        name="forward",
    )(*mats, *pieces, *halos, *shown)
    return got[0], got[1:]


def backward_kernel(cover, *refs):
    mats, center, halos, strips = refs[:6], refs[6], refs[7:11], refs[11:13]
    mine, other = refs[13:15]
    wide, across, logs, sems, out_sems = refs[15:]
    z, y, x, c = place()
    copies = Copies(sems)
    for q in range(4):
        copies.add(center.at[q], wide.at[pl.ds(1, 4), :, :, :, 1 + q])
        for n in range(2):
            copies.add(halos[n].at[q], wide.at[5 * n, :, :, :, 1 + q])
    for n in range(2, 4):
        copies.add(halos[n], halo_slot(wide, FACES[n]))
    for n, dy in enumerate((1, -1)):
        for m, dz in enumerate((1, -1)):
            copies.add(strips[n].at[m], halo_slot(wide, (dz, dy)))
    copies.wait()
    plane = z * 64 + lax.broadcasted_iota(jnp.int32, (64, 256), 0)
    inside = jnp.logical_and(plane >= cover[0, 0], plane < cover[0, 1])

    def finish(group, rows, value):
        store_halves(logs, group, rows, jnp.where(inside, jnp.log(value), jnp.float32(0.0)))

    blur(1, mats, wide, across, finish)
    copies = Copies(out_sems)
    for half in range(2):
        tile = grouped(logs, half)
        lanes = pl.ds(128 * half, 128)
        for q in range(4):
            copies.add(tile.at[q, :, 1 - c], other.at[:, :, :, q, :, lanes])
            copies.add(tile.at[q, :, c], mine.at[:, :, :, q, :, lanes])
    copies.wait()


def backward(cover, mats, center, halos, strips):
    half = jax.ShapeDtypeStruct((4,) + PART, F32)
    return pl.pallas_call(
        backward_kernel,
        out_shape=(half, half),
        in_specs=[SMEM] + [VMEM] * 6 + [ANY] * 7,
        out_specs=(ANY, ANY),
        scratch_shapes=[
            pltpu.VMEM(WIDE, F32),
            pltpu.VMEM((2, 4, 768, 128), F32),
            pltpu.VMEM((2, 4, 512, 128), F32),
            pltpu.SemaphoreType.DMA((18,)),
            pltpu.SemaphoreType.DMA((16,)),
        ],
        compiler_params=params(),
        name="backward",
    )(cover, *mats, center, *halos, *strips)


def shares_kernel(mine, got, *outs):
    z, y, x, c = place()
    for k in range(4):
        s = (x + k) % XD
        outs[k][...] = mine[:, s] + got[:, s]


def shares(mine, got):
    part = jax.ShapeDtypeStruct(PART, F32)
    return pl.pallas_call(
        shares_kernel,
        out_shape=(part,) * 4,
        in_specs=[VMEM, VMEM],
        out_specs=(VMEM,) * 4,
        compiler_params=params(),
        name="shares",
    )(mine, got)


def edges_kernel(*refs):
    pieces, outs = refs[:8], refs[8:12]
    tile, sems, out_sems = refs[12:]
    z, y, x, c = place()
    copies = Copies(sems)
    put_pieces(copies, pieces, lambda h, s: tile.at[:, h, s], x, c)
    copies.wait()
    copies = Copies(out_sems)
    for n, (step0, step1) in enumerate(STEPS):
        out1 = outs[n].reshape(*YEDGE) if n < 2 else outs[n]
        copies.add_by_core(c, (edge_of(tile, step0), outs[n]), (edge_of(tile, step1), out1))
    copies.wait()


def edges(pieces):
    return pl.pallas_call(
        edges_kernel,
        out_shape=tuple(jax.ShapeDtypeStruct(s, F32) for s in (ZEDGE, ZEDGE, CORNER, CORNER)),
        in_specs=[ANY] * 8,
        out_specs=(ANY,) * 4,
        scratch_shapes=[
            pltpu.VMEM(TILE, F32),
            pltpu.SemaphoreType.DMA((8,)),
            pltpu.SemaphoreType.DMA((4,)),
        ],
        compiler_params=params(),
        name="edges",
    )(*pieces)


def slab_kernel(*refs):
    pieces, out = refs[:8], refs[8]
    slab, sems, out_sems = refs[9:]
    z, y, x, c = place()
    copies = Copies(sems)
    put_pieces(copies, pieces, lambda h, s: slab.at[h, s], x, c)
    copies.wait()
    copies = Copies(out_sems)
    copies.add(slab, out)
    copies.wait()


def slab(pieces):
    return pl.pallas_call(
        slab_kernel,
        out_shape=jax.ShapeDtypeStruct((2, 4, 2, 128, 256), F32),
        in_specs=[ANY] * 8,
        out_specs=ANY,
        scratch_shapes=[
            pltpu.VMEM((2, 4, 2, 128, 256), F32),
            pltpu.SemaphoreType.DMA((8,)),
            pltpu.SemaphoreType.DMA((1,)),
        ],
        compiler_params=params(),
        name="slab",
    )(*pieces)


def by_block(pieces, y):
    order = [pieces[0], pieces[3], pieces[2], pieces[1]]
    stack = jnp.stack(order + order[:3])
    return lax.dynamic_slice_in_dim(stack, (YD - y) % YD, 4, axis=0)


def gathered(share):
    return [share] + [x_turn(share, k) for k in (1, 2, 3)]


def local(estimate, views, axial_taps, lateral_taps, cover):
    z, y, x, c = place()

    def rows_for(value, k, axis):
        return lax.dynamic_slice_in_dim(value, 32 * ((y + k) % YD), 32, axis=axis)

    own = lax.dynamic_slice_in_dim(estimate, 8 * c + 2 * x, 2, axis=0)
    parts = [rows_for(own, 0, 1)] + [y_turn(rows_for(own, k, 1), k) for k in (1, 2, 3)]
    share = by_block(parts, y).reshape(PART)
    mats = matrices(axial_taps, lateral_taps)
    def view_rows(k):
        rows = lax.dynamic_slice_in_dim(views[0].reshape(16, 16, 8, 256), 4 * ((y + k) % YD), 4, axis=1)
        return jnp.transpose(rows, (1, 0, 2, 3)).reshape(4, 2, 4, 2, 8, 256)

    shown = [view_rows(k) for k in range(4)]
    share, *rest = lax.optimization_barrier((share, *mats, *shown))
    mats, shown = rest[:6], rest[6:]
    shown = [shown[0]] + [y_turn(shown[k], k) for k in (1, 2, 3)]
    for step in range(ITERS):
        pieces = gathered(share)
        pieces = pieces + [core_swap(piece) for piece in pieces]
        if step == 0:
            pieces, shown = lax.optimization_barrier((pieces, shown))
        halos = []
        rims = [core_step(edge, steps) for edge, steps in zip(edges(pieces), STEPS)]
        rims = lax.optimization_barrier(rims)
        for n, moved in enumerate(rims):
            for value in (moved, core_swap(moved)):
                halos += [value, value.reshape(YEDGE)] if n < 2 else [value]
        center, rims = forward(mats, pieces, halos, shown)
        halos = [blk_shift(e, *d) for e, d in zip(rims, FACES)]
        low, high = halos[0], halos[1]
        strips = [blk_shift(jnp.stack([low[r], high[r]]), 0, dy) for r, dy in ((3, 1), (0, -1))]
        mine, other = backward(cover, mats, center, halos, strips)
        terms = shares(mine, core_swap(other))
        total = terms[0]
        for k in (1, 2, 3):
            total = total + x_turn(terms[k], k)
        share = share * jnp.exp(total)
    share = share.reshape(4, 2, 32, 256)
    parts = [lax.dynamic_index_in_dim(share, (y + k) % YD, 0, keepdims=False) for k in range(4)]
    parts = [parts[0]] + [y_turn(parts[k], k) for k in (1, 2, 3)]
    strip = by_block(parts, y)
    strip = jnp.transpose(strip, (1, 0, 2, 3)).reshape(2, 128, 256)
    pieces = gathered(strip)
    pieces = pieces + [core_swap(piece) for piece in pieces]
    return slab(pieces).reshape(16, 128, 256)


def solution(mesh):
    in_specs = (
        P("blk", None, None),
        P("view", "blk", None, None),
        P("view", None),
        P("view", None, None),
        P("view", None),
    )
    out_specs = P("blk", None, None)
    return jax.shard_map(local, mesh=mesh, in_specs=in_specs, out_specs=out_specs, check_vma=False)
```

```python
import functools

import jax
import jax.numpy as jnp
from jax import lax
from jax.experimental import pallas as pl
from jax.experimental.pallas import tpu as pltpu
from jax.sharding import PartitionSpec as P

RAD = 8
RZ = 16
ITERS = 2
YD = 4
XD = 4
F32 = jnp.float32
BF16 = jnp.bfloat16
NLAT = 2 * RAD + 1
NAX = 2 * RZ + 1

ANY = pl.BlockSpec(memory_space=pl.ANY)
SMEM = pl.BlockSpec(memory_space=pltpu.SMEM)
VMEM = pl.BlockSpec(memory_space=pltpu.VMEM)
STEPS = (((1, 0), (0, 1)), ((-1, 0), (0, -1)), ((1, 1), (1, -1)), ((-1, -1), (-1, 1)))


def params():
    return pltpu.CompilerParams(vmem_limit_bytes=56 * 1024 * 1024)


def blk_shift(value, dz, dy):
    count = lax.axis_size("blk") // YD
    pairs = [
        (z * YD + y, (z + dz) * YD + y + dy)
        for z in range(count)
        for y in range(YD)
        if 0 <= z + dz < count and 0 <= y + dy < YD
    ]
    return lax.ppermute(value, "blk", pairs)


def core_step(value, steps):
    count = lax.axis_size("blk") // YD
    views = lax.axis_size("view")
    pairs = []
    for z in range(count):
        for y in range(YD):
            for v in range(views):
                dz, dy = steps[v % 2]
                if 0 <= z + dz < count and 0 <= y + dy < YD:
                    target = (z + dz) * YD + y + dy
                    pairs.append(((z * YD + y) * views + v, target * views + v))
    return lax.ppermute(value, ("blk", "view"), pairs)


def y_turn(value, k):
    count = lax.axis_size("blk") // YD
    pairs = [(z * YD + y, z * YD + (y + k) % YD) for z in range(count) for y in range(YD)]
    return lax.ppermute(value, "blk", pairs)


def x_turn(value, k):
    pairs = [(2 * x + c, 2 * ((x + k) % XD) + c) for x in range(XD) for c in range(2)]
    return lax.ppermute(value, "view", pairs)


def core_swap(value):
    return lax.ppermute(value, "view", [(i, i ^ 1) for i in range(2 * XD)])


def split(value):
    high = value.astype(BF16)
    return high, (value - high.astype(F32)).astype(BF16)


def mm(a, b):
    return jnp.dot(a, b, preferred_element_type=F32)


def matrices_kernel(axial_taps, lateral_taps, kyh, kyl, kxh, kxl, kzh, kzl):
    one = jnp.int32(1)
    zero = jnp.int32(0)

    def iota(shape, axis):
        return lax.broadcasted_iota(jnp.int32, shape, axis)

    def near(shape, start):
        row, col = iota(shape, 0), iota(shape, 1)
        pcol = sum(jnp.where(col >= 48 * n, one, zero) for n in (1, 2, 3))
        return jnp.where(pcol == start // 32, (col - 48 * pcol) - (row + start % 32), -1)

    def wide(shape, start):
        return iota(shape, 0) + start - iota(shape, 1) + RAD

    def deep(shape, start):
        return iota(shape, 1) - iota(shape, 0) - start

    def fill(where, tap, count, high, low):
        taps = [tap(d) for d in range(count)]
        norm = sum(taps[1:], taps[0])
        shape = (16, high.shape[2])

        @pl.loop(0, high.shape[1] // 16)
        def _(n):
            start = pl.multiple_of(16 * n, 16)
            offset = where(shape, start)
            for way in range(2):
                matrix = jnp.zeros(shape, F32)
                for d in range(count):
                    matrix = jnp.where(offset == (d if way == 0 else count - 1 - d), taps[d], matrix)
                matrix = matrix / jnp.full(shape, norm)
                high[way, pl.ds(start, 16)], low[way, pl.ds(start, 16)] = split(matrix)

    fill(near, lambda d: lateral_taps[0, 0, d], NLAT, kyh, kyl)
    fill(wide, lambda d: lateral_taps[0, 1, d], NLAT, kxh, kxl)
    fill(deep, lambda d: axial_taps[0, d], NAX, kzh, kzl)


def matrices(axial_taps, lateral_taps):
    ky = jax.ShapeDtypeStruct((2, 128, 192), BF16)
    kx = jax.ShapeDtypeStruct((2, 256, 256), BF16)
    kz = jax.ShapeDtypeStruct((2, 64, 96), BF16)
    return pl.pallas_call(
        matrices_kernel,
        out_shape=(ky, ky, kx, kx, kz, kz),
        in_specs=[SMEM, SMEM],
        out_specs=(VMEM,) * 6,
        compiler_params=params(),
        name="matrices",
    )(axial_taps, lateral_taps)


def both_halves(ref, group, rows):
    return jnp.concatenate([ref[0, group, rows, :], ref[1, group, rows, :]], axis=1)


def store_halves(ref, group, rows, value):
    ref[0, group, rows, :] = value[:, :128]
    ref[1, group, rows, :] = value[:, 128:]


def blur(way, mats, wide, across, inner, outer, ready, finish, done):
    kyh, kyl, kxh, kxl, kzh, kzl = [m[way] for m in mats]

    def over_rows(b):
        for n in range(4):
            block = wide[b, n // 2, pl.ds(2 * (n % 2), 2)].reshape(192, 256)
            high, low = split(block)
            rows = mm(kyh, high) + (mm(kyl, high) + mm(kyh, low))
            for p in range(4):
                at = pl.ds(pl.multiple_of(128 * b + 32 * n + 8 * p, 8), 8)
                for q in range(4):
                    store_halves(across, q, at, rows[32 * p + 8 * q : 32 * p + 8 * q + 8])

    inner()
    pl.loop(1, 5)(over_rows)
    outer()
    pl.loop(0, 2)(lambda n: over_rows(5 * n))
    ready()

    @pl.loop(0, 8)
    def _(n):
        q = n // 2
        r0 = 4 * (n % 2)
        deep = []
        for r in range(4):
            high, low = split(both_halves(across, q, pl.ds(r0 + r, 96, stride=8)))
            deep.append(mm(kzh, high) + (mm(kzl, high) + mm(kzh, low)))
        high, low = split(jnp.concatenate(deep, axis=0))
        both = mm(high, kxh) + (mm(low, kxh) + mm(high, kxl))
        for r in range(4):
            finish(q, pl.ds(r0 + r, 64, stride=8), both[64 * r : 64 * r + 64])

        @pl.when(r0 > 0)
        def _():
            done(q)


def halo_slot(wide, step):
    dz, dy = step
    b = {1: 0, -1: 5, 0: pl.ds(1, 4)}[dz]
    r = {1: 0, -1: 5, 0: pl.ds(1, 4)}[dy]
    return wide.at[b, :, :, :, r]


def edge_of(tile, step):
    dz, dy = step
    b = {-1: 0, 1: 3, 0: pl.ds(0, 4)}[dz]
    r = {-1: 0, 1: 3, 0: pl.ds(0, 4)}[dy]
    return tile.at[b, :, :, :, r]


def place():
    blk = lax.axis_index("blk")
    view = lax.axis_index("view")
    return blk // YD, blk % YD, view // 2, view % 2


class Copies:
    def __init__(self, sems):
        self.sems = sems
        self.items = []

    def add(self, source, target):
        item = pltpu.make_async_copy(source, target, self.sems.at[len(self.items)])
        item.start()
        self.items.append(item)
        return len(self.items)

    def add_by_core(self, c, pair0, pair1):
        items = [pltpu.make_async_copy(*p, self.sems.at[len(self.items)]) for p in (pair0, pair1)]
        pl.when(c == 0)(items[0].start)
        pl.when(c != 0)(items[1].start)
        self.items.append(items[0])

    def wait(self, first=0, end=None):
        for item in self.items[first:end]:
            item.wait()


TILE = (4, 2, 4, 2, 4, 8, 256)
WIDE = (6, 2, 4, 2, 6, 8, 256)
ZEDGE = (2, 4, 2, 4, 8, 256)
YEDGE = (4, 2, 4, 2, 8, 256)
CORNER = (2, 4, 2, 8, 256)
PART = (4, 2, 4, 8, 256)
RATIO = (4, 4, 2, 4, 2, 8, 256)
RATIO_ZEDGE = (4, 2, 4, 2, 8, 256)
FACES = ((1, 0), (-1, 0), (0, 1), (0, -1))


def grouped(ref, half):
    return ref.at[half].reshape(4, 4, 2, 4, 2, 8, 128)


def put_pieces(copies, first, pieces, tile):
    z, y, x, c = place()
    for k in range(4):
        for other in range(2):
            half = c if other == 0 else 1 - c
            if first:
                slot = tile((y - k + YD) % YD, half, pl.ds(0, 4))
            else:
                slot = tile(pl.ds(0, 4), half, (x - k + XD) % XD)
            copies.add(pieces[4 * other + k], slot)


def forward_kernel(first, *refs):
    mats, pieces, moved, got, shown = refs[:6], refs[6:14], refs[14:18], refs[18], refs[19:23]
    center, edges = refs[23], refs[24:28]
    wide, across, views, ratio, sems, group_sems, out_sems = refs[28:]
    z, y, x, c = place()
    copies = Copies(sems)
    middle = wide.at[pl.ds(1, 4)]
    put_pieces(copies, first, pieces, lambda b, h, s: middle.at[b, h, s, :, pl.ds(1, 4)])
    for n, (step0, step1) in enumerate(STEPS):
        shapes = (ZEDGE, YEDGE) if n < 2 else (CORNER, CORNER)
        start, size = ((64 * n, 64) if n < 2 else (96 + 16 * n, 16))
        theirs = got.at[pl.ds(start, size)]
        slot0, slot1 = halo_slot(wide, step0), halo_slot(wide, step1)
        copies.add_by_core(c, (moved[n], slot0), (theirs.reshape(*shapes[0]), slot0))
        copies.add_by_core(c, (theirs.reshape(*shapes[1]), slot1), (moved[n].reshape(*shapes[1]), slot1))
    count = len(copies.items)
    for k in range(4):
        b = (y - k + YD) % YD
        for half in range(2):
            copies.add(shown[k].at[..., pl.ds(128 * half, 128)], grouped(views, half).at[:, b])

    def finish(group, rows, value):
        store_halves(ratio, group, rows, both_halves(views, group, rows) / value)

    def group_copies(q):
        for half in range(2):
            tile = grouped(ratio, half).at[q]
            lanes = pl.ds(128 * half, 128)
            for n, (source, target) in enumerate(((3, edges[0]), (0, edges[1]), (None, center))):
                source = tile if source is None else tile.at[source]
                yield pltpu.make_async_copy(source, target.at[q, ..., lanes], group_sems.at[q, half, n])

    def done(q):
        for item in group_copies(q):
            item.start()

    blur(
        0,
        mats,
        wide,
        across,
        lambda: copies.wait(0, count),
        lambda: None,
        lambda: copies.wait(count),
        finish,
        done,
    )
    copies = Copies(out_sems)
    for half in range(2):
        tile = grouped(ratio, half)
        lanes = pl.ds(128 * half, 128)
        for n, edge in ((2, tile.at[3]), (3, tile.at[0])):
            copies.add(edge, edges[n].at[..., lanes])
    for q in range(4):
        for item in group_copies(q):
            item.wait()
    copies.wait()


def forward(first, mats, pieces, moved, got, shown):
    shapes = (RATIO, RATIO_ZEDGE, RATIO_ZEDGE, YEDGE, YEDGE)
    got = pl.pallas_call(
        functools.partial(forward_kernel, first),
        out_shape=tuple(jax.ShapeDtypeStruct(s, F32) for s in shapes),
        in_specs=[VMEM] * 6 + [ANY] * 17,
        out_specs=(ANY,) * 5,
        scratch_shapes=[
            pltpu.VMEM(WIDE, F32),
            pltpu.VMEM((2, 4, 768, 128), F32),
            pltpu.VMEM((2, 4, 512, 128), F32),
            pltpu.VMEM((2, 4, 512, 128), F32),
            pltpu.SemaphoreType.DMA((24,)),
            pltpu.SemaphoreType.DMA((4, 2, 3)),
            pltpu.SemaphoreType.DMA((4,)),
        ],
        compiler_params=params(),
        name="forward",
    )(*mats, *pieces, *moved, got, *shown)
    return got[0], got[1:]


def backward_kernel(cover, *refs):
    mats, center, halos, strips = refs[:6], refs[6], refs[7:11], refs[11:13]
    mine, other = refs[13:15]
    wide, across, logs, sems, out_sems = refs[15:]
    z, y, x, c = place()
    copies = Copies(sems)
    for n in range(2, 4):
        copies.add(halos[n], halo_slot(wide, FACES[n]))
    for q in range(4):
        count = copies.add(center.at[q], wide.at[pl.ds(1, 4), :, :, :, 1 + q])
    for q in range(4):
        for n in range(2):
            copies.add(halos[n].at[q], wide.at[5 * n, :, :, :, 1 + q])
    for n, dy in enumerate((1, -1)):
        for m, dz in enumerate((1, -1)):
            copies.add(strips[n].at[m], halo_slot(wide, (dz, dy)))
    plane = z * 64 + lax.broadcasted_iota(jnp.int32, (64, 256), 0)
    inside = jnp.logical_and(plane >= cover[0, 0], plane < cover[0, 1])

    def finish(group, rows, value):
        store_halves(logs, group, rows, jnp.where(inside, jnp.log(value), jnp.float32(0.0)))

    def group_copies(q):
        for half in range(2):
            tile = grouped(logs, half).at[q]
            lanes = pl.ds(128 * half, 128)
            for n, (core, target) in enumerate(((1 - c, other), (c, mine))):
                target = target.at[:, :, :, q, :, lanes]
                yield pltpu.make_async_copy(tile.at[:, core], target, out_sems.at[q, half, n])

    def done(q):
        for item in group_copies(q):
            item.start()

    blur(
        1,
        mats,
        wide,
        across,
        lambda: copies.wait(0, count),
        lambda: copies.wait(count),
        lambda: None,
        finish,
        done,
    )
    for q in range(4):
        for item in group_copies(q):
            item.wait()


def backward(cover, mats, center, halos, strips):
    half = jax.ShapeDtypeStruct((4,) + PART, F32)
    return pl.pallas_call(
        backward_kernel,
        out_shape=(half, half),
        in_specs=[SMEM] + [VMEM] * 6 + [ANY] * 7,
        out_specs=(ANY, ANY),
        scratch_shapes=[
            pltpu.VMEM(WIDE, F32),
            pltpu.VMEM((2, 4, 768, 128), F32),
            pltpu.VMEM((2, 4, 512, 128), F32),
            pltpu.SemaphoreType.DMA((18,)),
            pltpu.SemaphoreType.DMA((4, 2, 2)),
        ],
        compiler_params=params(),
        name="backward",
    )(cover, *mats, center, *halos, *strips)


def shares_kernel(mine, got, *outs):
    z, y, x, c = place()
    for k in range(4):
        s = (x + k) % XD
        outs[k][...] = mine[:, s] + got[:, s]


def shares(mine, got):
    part = jax.ShapeDtypeStruct(PART, F32)
    return pl.pallas_call(
        shares_kernel,
        out_shape=(part,) * 4,
        in_specs=[VMEM, VMEM],
        out_specs=(VMEM,) * 4,
        compiler_params=params(),
        name="shares",
    )(mine, got)


def edges_kernel(first, *refs):
    pieces, outs = refs[:8], refs[8:12]
    tile, sems, out_sems = refs[12:]
    z, y, x, c = place()
    copies = Copies(sems)
    put_pieces(copies, first, pieces, lambda b, h, s: tile.at[b, h, s])
    copies.wait()
    copies = Copies(out_sems)
    for n, (step0, step1) in enumerate(STEPS):
        out1 = outs[n].reshape(*YEDGE) if n < 2 else outs[n]
        copies.add_by_core(c, (edge_of(tile, step0), outs[n]), (edge_of(tile, step1), out1))
    copies.wait()


def edges(first, pieces):
    return pl.pallas_call(
        functools.partial(edges_kernel, first),
        out_shape=tuple(jax.ShapeDtypeStruct(s, F32) for s in (ZEDGE, ZEDGE, CORNER, CORNER)),
        in_specs=[ANY] * 8,
        out_specs=(ANY,) * 4,
        scratch_shapes=[
            pltpu.VMEM(TILE, F32),
            pltpu.SemaphoreType.DMA((8,)),
            pltpu.SemaphoreType.DMA((4,)),
        ],
        compiler_params=params(),
        name="edges",
    )(*pieces)


def slab_kernel(*refs):
    pieces, out = refs[:8], refs[8]
    slab, sems, out_sems = refs[9:]
    z, y, x, c = place()
    copies = Copies(sems)
    put_pieces(copies, False, pieces, lambda b, h, s: slab.at[h, s])
    copies.wait()
    copies = Copies(out_sems)
    copies.add(slab, out)
    copies.wait()


def slab(pieces):
    return pl.pallas_call(
        slab_kernel,
        out_shape=jax.ShapeDtypeStruct((2, 4, 2, 128, 256), F32),
        in_specs=[ANY] * 8,
        out_specs=ANY,
        scratch_shapes=[
            pltpu.VMEM((2, 4, 2, 128, 256), F32),
            pltpu.SemaphoreType.DMA((8,)),
            pltpu.SemaphoreType.DMA((1,)),
        ],
        compiler_params=params(),
        name="slab",
    )(*pieces)


def by_block(pieces, y):
    order = [pieces[0], pieces[3], pieces[2], pieces[1]]
    stack = jnp.stack(order + order[:3])
    return lax.dynamic_slice_in_dim(stack, (YD - y) % YD, 4, axis=0)


def gathered(share):
    return [share] + [x_turn(share, k) for k in (1, 2, 3)]


def local(estimate, views, axial_taps, lateral_taps, cover):
    z, y, x, c = place()

    def est_rows(k):
        half = lax.dynamic_slice_in_dim(estimate, 8 * c, 8, axis=0)
        rows = lax.dynamic_slice_in_dim(half, 32 * ((y + k) % YD), 32, axis=1)
        return rows.reshape(PART)

    def view_rows(k):
        rows = lax.dynamic_slice_in_dim(views[0].reshape(16, 16, 8, 256), 4 * ((y + k) % YD), 4, axis=1)
        return jnp.transpose(rows, (1, 0, 2, 3)).reshape(4, 2, 4, 2, 8, 256)

    pieces = [est_rows(0)] + [y_turn(est_rows(k), k) for k in (1, 2, 3)]
    share = by_block([lax.dynamic_index_in_dim(p, x, 0, keepdims=False) for p in pieces], y)
    mats = matrices(axial_taps, lateral_taps)
    shown = [view_rows(k) for k in range(4)]
    pieces, mats, shown = lax.optimization_barrier((pieces, mats, shown))
    shown = [shown[0]] + [y_turn(shown[k], k) for k in (1, 2, 3)]
    for step in range(ITERS):
        if step > 0:
            pieces = gathered(share)
        pieces = pieces + [core_swap(piece) for piece in pieces]
        rims = [core_step(e, steps) for e, steps in zip(edges(step == 0, pieces), STEPS)]
        if step == 0:
            rims, shown = lax.optimization_barrier((rims, shown))
        swapped = core_swap(jnp.concatenate([rim.reshape(-1, 8, 256) for rim in rims]))
        center, rims = forward(step == 0, mats, pieces, rims, swapped, shown)
        halos = [blk_shift(e, *d) for e, d in zip(rims, FACES)]
        low, high = halos[0], halos[1]
        strips = [blk_shift(jnp.stack([low[r], high[r]]), 0, dy) for r, dy in ((3, 1), (0, -1))]
        mine, other = backward(cover, mats, center, halos, strips)
        terms = shares(mine, core_swap(other))
        total = terms[0]
        for k in (1, 2, 3):
            total = total + x_turn(terms[k], k)
        share = share * jnp.exp(total)
    share = share.reshape(4, 2, 32, 256)
    parts = [lax.dynamic_index_in_dim(share, (y + k) % YD, 0, keepdims=False) for k in range(4)]
    parts = [parts[0]] + [y_turn(parts[k], k) for k in (1, 2, 3)]
    strip = by_block(parts, y)
    strip = jnp.transpose(strip, (1, 0, 2, 3)).reshape(2, 128, 256)
    pieces = gathered(strip)
    pieces = pieces + [core_swap(piece) for piece in pieces]
    return slab(pieces).reshape(16, 128, 256)


def solution(mesh):
    in_specs = (
        P("blk", None, None),
        P("view", "blk", None, None),
        P("view", None),
        P("view", None, None),
        P("view", None),
    )
    out_specs = P("blk", None, None)
    return jax.shard_map(local, mesh=mesh, in_specs=in_specs, out_specs=out_specs, check_vma=False)
```

```python
import functools

import jax
import jax.numpy as jnp
from jax import lax
from jax.experimental import pallas as pl
from jax.experimental.pallas import tpu as pltpu
from jax.sharding import PartitionSpec as P

RAD = 8
RZ = 16
ITERS = 2
YD = 4
XD = 4
F32 = jnp.float32
BF16 = jnp.bfloat16
NLAT = 2 * RAD + 1
NAX = 2 * RZ + 1

ANY = pl.BlockSpec(memory_space=pl.ANY)
SMEM = pl.BlockSpec(memory_space=pltpu.SMEM)
VMEM = pl.BlockSpec(memory_space=pltpu.VMEM)
STEPS = (((1, 0), (0, 1)), ((-1, 0), (0, -1)), ((1, 1), (1, -1)), ((-1, -1), (-1, 1)))


def params():
    return pltpu.CompilerParams(vmem_limit_bytes=56 * 1024 * 1024)


def blk_shift(value, dz, dy):
    count = lax.axis_size("blk") // YD
    pairs = [
        (z * YD + y, (z + dz) * YD + y + dy)
        for z in range(count)
        for y in range(YD)
        if 0 <= z + dz < count and 0 <= y + dy < YD
    ]
    return lax.ppermute(value, "blk", pairs)


def core_step(value, steps):
    count = lax.axis_size("blk") // YD
    views = lax.axis_size("view")
    pairs = []
    for z in range(count):
        for y in range(YD):
            for v in range(views):
                dz, dy = steps[v % 2]
                if 0 <= z + dz < count and 0 <= y + dy < YD:
                    target = (z + dz) * YD + y + dy
                    pairs.append(((z * YD + y) * views + v, target * views + v))
    return lax.ppermute(value, ("blk", "view"), pairs)


def y_turn(value, k):
    count = lax.axis_size("blk") // YD
    pairs = [(z * YD + y, z * YD + (y + k) % YD) for z in range(count) for y in range(YD)]
    return lax.ppermute(value, "blk", pairs)


def x_turn(value, k):
    pairs = [(2 * x + c, 2 * ((x + k) % XD) + c) for x in range(XD) for c in range(2)]
    return lax.ppermute(value, "view", pairs)


def core_swap(value):
    return lax.ppermute(value, "view", [(i, i ^ 1) for i in range(2 * XD)])


def split(value):
    high = value.astype(BF16)
    return high, (value - high.astype(F32)).astype(BF16)


def mm(a, b):
    return jnp.dot(a, b, preferred_element_type=F32)


def matrices_kernel(axial_taps, lateral_taps, ky, kzh, kzl, kxh, kxl):
    one = jnp.int32(1)
    zero = jnp.int32(0)

    def iota(shape, axis):
        return lax.broadcasted_iota(jnp.int32, shape, axis)

    def fill(shape, offset, tap, count, put):
        taps = [tap(d) for d in range(count)]
        norm = sum(taps[1:], taps[0])

        @pl.loop(0, shape[0] // 16)
        def _(n):
            start = pl.multiple_of(16 * n, 16)
            where = offset((16, shape[1]), start)
            for way in range(2):
                matrix = jnp.zeros((16, shape[1]), F32)
                for d in range(count):
                    matrix = jnp.where(where == (d if way == 0 else count - 1 - d), taps[d], matrix)
                put(way, pl.ds(start, 16), split(matrix / jnp.full((16, shape[1]), norm)))

    def three(depth, out):
        def part(shape):
            col = iota(shape, 1)
            return jnp.where(col >= depth, one, zero) + jnp.where(col >= 2 * depth, one, zero)

        def offset(shape, start):
            return iota(shape, 1) - depth * part(shape) - iota(shape, 0) - start

        def put(way, rows, parts):
            high, low = [value.astype(F32) for value in parts]
            out[way, rows] = jnp.where(part(high.shape) == 1, low, high).astype(BF16)

        return (32, 3 * depth), offset, put

    def wide(shape, start):
        return iota(shape, 0) + start - iota(shape, 1) + RAD

    def put_wide(way, rows, parts):
        kxh[way, rows], kxl[way, rows] = parts

    shape, offset, put = three(32 + 2 * RAD, ky)
    fill(shape, offset, lambda d: lateral_taps[0, 0, d], NLAT, put)
    fill((256, 256), wide, lambda d: lateral_taps[0, 1, d], NLAT, put_wide)

    def deep(shape, start):
        return iota(shape, 1) - iota(shape, 0) - start

    def put_deep(way, rows, parts):
        kzh[way, rows], kzl[way, rows] = parts

    fill((64, 96), deep, lambda d: axial_taps[0, d], NAX, put_deep)


def matrices(axial_taps, lateral_taps):
    ky = jax.ShapeDtypeStruct((2, 32, 144), BF16)
    kz = jax.ShapeDtypeStruct((2, 64, 96), BF16)
    kx = jax.ShapeDtypeStruct((2, 256, 256), BF16)
    return pl.pallas_call(
        matrices_kernel,
        out_shape=(ky, kz, kz, kx, kx),
        in_specs=[SMEM, SMEM],
        out_specs=(VMEM,) * 5,
        compiler_params=params(),
        name="matrices",
    )(axial_taps, lateral_taps)


def both_halves(ref, group, rows):
    return jnp.concatenate([ref[0, group, rows, :], ref[1, group, rows, :]], axis=1)


def store_halves(ref, group, rows, value):
    ref[0, group, rows, :] = value[:, :128]
    ref[1, group, rows, :] = value[:, 128:]


def three_products(matrix, high, low):
    return mm(matrix, jnp.concatenate([high, high, low], axis=0))


def blur(way, mats, wide, across, inner, outer, ready, finish, done):
    ky, kzh, kzl, kxh, kxl = [m[way] for m in mats]

    def over_rows(b):
        for n in range(16):
            block = wide[b, n // 8, (n // 2) % 4, n % 2].reshape(48, 256)
            rows = three_products(ky, *split(block))
            at = pl.ds(pl.multiple_of(128 * b + 8 * n, 8), 8)
            for q in range(4):
                store_halves(across, q, at, rows[8 * q : 8 * q + 8])

    inner()
    pl.loop(1, 5)(over_rows)
    outer()
    pl.loop(0, 2)(lambda n: over_rows(5 * n))
    ready()

    @pl.loop(0, 8)
    def _(n):
        q = n // 2
        r0 = 4 * (n % 2)
        deep = []
        for r in range(4):
            high, low = split(both_halves(across, q, pl.ds(r0 + r, 96, stride=8)))
            deep.append(mm(kzh, high) + (mm(kzl, high) + mm(kzh, low)))
        high, low = split(jnp.concatenate(deep, axis=0))
        both = mm(high, kxh) + (mm(low, kxh) + mm(high, kxl))
        for r in range(4):
            finish(q, pl.ds(r0 + r, 64, stride=8), both[64 * r : 64 * r + 64])

        @pl.when(r0 > 0)
        def _():
            done(q)


def halo_slot(wide, step):
    dz, dy = step
    b = {1: 0, -1: 5, 0: pl.ds(1, 4)}[dz]
    r = {1: 0, -1: 5, 0: pl.ds(1, 4)}[dy]
    return wide.at[b, :, :, :, r]


def edge_of(tile, step):
    dz, dy = step
    b = {-1: 0, 1: 3, 0: pl.ds(0, 4)}[dz]
    r = {-1: 0, 1: 3, 0: pl.ds(0, 4)}[dy]
    return tile.at[b, :, :, :, r]


def place():
    blk = lax.axis_index("blk")
    view = lax.axis_index("view")
    return blk // YD, blk % YD, view // 2, view % 2


class Copies:
    def __init__(self, sems):
        self.sems = sems
        self.items = []

    def add(self, source, target):
        item = pltpu.make_async_copy(source, target, self.sems.at[len(self.items)])
        item.start()
        self.items.append(item)
        return len(self.items)

    def add_by_core(self, c, pair0, pair1):
        items = [pltpu.make_async_copy(*p, self.sems.at[len(self.items)]) for p in (pair0, pair1)]
        pl.when(c == 0)(items[0].start)
        pl.when(c != 0)(items[1].start)
        self.items.append(items[0])

    def wait(self, first=0, end=None):
        for item in self.items[first:end]:
            item.wait()


TILE = (4, 2, 4, 2, 4, 8, 256)
WIDE = (6, 2, 4, 2, 6, 8, 256)
ZEDGE = (2, 4, 2, 4, 8, 256)
YEDGE = (4, 2, 4, 2, 8, 256)
CORNER = (2, 4, 2, 8, 256)
PART = (4, 2, 4, 8, 256)
RATIO = (4, 4, 2, 4, 2, 8, 256)
RATIO_ZEDGE = (4, 2, 4, 2, 8, 256)
FACES = ((1, 0), (-1, 0), (0, 1), (0, -1))


def grouped(ref, half):
    return ref.at[half].reshape(4, 4, 2, 4, 2, 8, 128)


def put_pieces(copies, pieces, tile):
    z, y, x, c = place()
    for k in range(4):
        s = (x - k + XD) % XD
        for other in range(2):
            half = c if other == 0 else 1 - c
            copies.add(pieces[4 * other + k], tile(half, s))


def forward_kernel(first, *refs):
    inputs = 17 if first else 18
    mats, tile, refs = refs[:5], refs[5:inputs], refs[inputs:]
    shown, center, edges = refs[:4], refs[4], refs[5:9]
    wide, across, views, ratio, sems, group_sems, out_sems = refs[9:]
    z, y, x, c = place()
    copies = Copies(sems)
    middle = wide.at[pl.ds(1, 4)]
    if first:
        for other in range(2):
            half = c if other == 0 else 1 - c
            for k in range(4):
                copies.add(tile[4 * other + k], middle.at[(y - k + YD) % YD, half])
            for n in range(2):
                copies.add(tile[8 + 2 * other + n], wide.at[5 * n, half])
    else:
        pieces, moved, got = tile[:8], tile[8:12], tile[12]
        put_pieces(copies, pieces, lambda h, s: middle.at[:, h, s, :, pl.ds(1, 4)])
        for n, (step0, step1) in enumerate(STEPS):
            shapes = (ZEDGE, YEDGE) if n < 2 else (CORNER, CORNER)
            start, size = (64 * n, 64) if n < 2 else (96 + 16 * n, 16)
            theirs = got.at[pl.ds(start, size)]
            slot0, slot1 = halo_slot(wide, step0), halo_slot(wide, step1)
            copies.add_by_core(c, (moved[n], slot0), (theirs.reshape(*shapes[0]), slot0))
            own = moved[n].reshape(*shapes[1])
            copies.add_by_core(c, (theirs.reshape(*shapes[1]), slot1), (own, slot1))
    count = len(copies.items)
    for k in range(4):
        b = (y - k + YD) % YD
        for half in range(2):
            copies.add(shown[k].at[..., pl.ds(128 * half, 128)], grouped(views, half).at[:, b])

    def finish(group, rows, value):
        store_halves(ratio, group, rows, both_halves(views, group, rows) / value)

    def group_copies(q):
        for half in range(2):
            tile = grouped(ratio, half).at[q]
            lanes = pl.ds(128 * half, 128)
            for n, (source, target) in enumerate(((3, edges[0]), (0, edges[1]), (None, center))):
                source = tile if source is None else tile.at[source]
                yield pltpu.make_async_copy(source, target.at[q, ..., lanes], group_sems.at[q, half, n])

    def done(q):
        for item in group_copies(q):
            item.start()

    blur(
        0,
        mats,
        wide,
        across,
        lambda: copies.wait(0, count),
        lambda: None,
        lambda: copies.wait(count),
        finish,
        done,
    )
    copies = Copies(out_sems)
    for half in range(2):
        tile = grouped(ratio, half)
        lanes = pl.ds(128 * half, 128)
        for n, edge in ((2, tile.at[3]), (3, tile.at[0])):
            copies.add(edge, edges[n].at[..., lanes])
    for q in range(4):
        for item in group_copies(q):
            item.wait()
    copies.wait()


def forward(first, mats, tile, shown):
    shapes = (RATIO, RATIO_ZEDGE, RATIO_ZEDGE, YEDGE, YEDGE)
    got = pl.pallas_call(
        functools.partial(forward_kernel, first),
        out_shape=tuple(jax.ShapeDtypeStruct(s, F32) for s in shapes),
        in_specs=[VMEM] * 5 + [ANY] * (len(tile) + 4),
        out_specs=(ANY,) * 5,
        scratch_shapes=[
            pltpu.VMEM(WIDE, F32),
            pltpu.VMEM((2, 4, 768, 128), F32),
            pltpu.VMEM((2, 4, 512, 128), F32),
            pltpu.VMEM((2, 4, 512, 128), F32),
            pltpu.SemaphoreType.DMA((24,)),
            pltpu.SemaphoreType.DMA((4, 2, 3)),
            pltpu.SemaphoreType.DMA((4,)),
        ],
        compiler_params=params(),
        name="forward",
    )(*mats, *tile, *shown)
    return got[0], got[1:]


def backward_kernel(cover, *refs):
    mats, center, halos, strips = refs[:5], refs[5], refs[6:10], refs[10:12]
    mine, other = refs[12:14]
    wide, across, logs, sems, out_sems = refs[14:]
    z, y, x, c = place()
    copies = Copies(sems)
    for n in range(2, 4):
        copies.add(halos[n], halo_slot(wide, FACES[n]))
    for q in range(4):
        count = copies.add(center.at[q], wide.at[pl.ds(1, 4), :, :, :, 1 + q])
    for q in range(4):
        for n in range(2):
            copies.add(halos[n].at[q], wide.at[5 * n, :, :, :, 1 + q])
    for n, dy in enumerate((1, -1)):
        for m, dz in enumerate((1, -1)):
            copies.add(strips[n].at[m], halo_slot(wide, (dz, dy)))
    plane = z * 64 + lax.broadcasted_iota(jnp.int32, (64, 256), 0)
    inside = jnp.logical_and(plane >= cover[0, 0], plane < cover[0, 1])

    def finish(group, rows, value):
        store_halves(logs, group, rows, jnp.where(inside, jnp.log(value), jnp.float32(0.0)))

    def group_copies(q):
        for half in range(2):
            tile = grouped(logs, half).at[q]
            lanes = pl.ds(128 * half, 128)
            for n, (core, target) in enumerate(((1 - c, other), (c, mine))):
                target = target.at[:, :, :, q, :, lanes]
                yield pltpu.make_async_copy(tile.at[:, core], target, out_sems.at[q, half, n])

    def done(q):
        for item in group_copies(q):
            item.start()

    blur(
        1,
        mats,
        wide,
        across,
        lambda: copies.wait(0, count),
        lambda: copies.wait(count),
        lambda: None,
        finish,
        done,
    )
    for q in range(4):
        for item in group_copies(q):
            item.wait()


def backward(cover, mats, center, halos, strips):
    half = jax.ShapeDtypeStruct((4,) + PART, F32)
    return pl.pallas_call(
        backward_kernel,
        out_shape=(half, half),
        in_specs=[SMEM] + [VMEM] * 5 + [ANY] * 7,
        out_specs=(ANY, ANY),
        scratch_shapes=[
            pltpu.VMEM(WIDE, F32),
            pltpu.VMEM((2, 4, 768, 128), F32),
            pltpu.VMEM((2, 4, 512, 128), F32),
            pltpu.SemaphoreType.DMA((18,)),
            pltpu.SemaphoreType.DMA((4, 2, 2)),
        ],
        compiler_params=params(),
        name="backward",
    )(cover, *mats, center, *halos, *strips)


def shares_kernel(mine, got, *outs):
    z, y, x, c = place()
    for k in range(4):
        s = (x + k) % XD

        @pl.loop(0, 4)
        def _(b):
            outs[k][b] = mine[b, s] + got[b, s]


def shares(mine, got):
    part = jax.ShapeDtypeStruct(PART, F32)
    return pl.pallas_call(
        shares_kernel,
        out_shape=(part,) * 4,
        in_specs=[VMEM, VMEM],
        out_specs=(VMEM,) * 4,
        compiler_params=params(),
        name="shares",
    )(mine, got)


def edges_kernel(*refs):
    pieces, outs = refs[:8], refs[8:12]
    tile, sems, out_sems = refs[12:]
    z, y, x, c = place()
    copies = Copies(sems)
    put_pieces(copies, pieces, lambda h, s: tile.at[:, h, s])
    copies.wait()
    copies = Copies(out_sems)
    for n, (step0, step1) in enumerate(STEPS):
        out1 = outs[n].reshape(*YEDGE) if n < 2 else outs[n]
        copies.add_by_core(c, (edge_of(tile, step0), outs[n]), (edge_of(tile, step1), out1))
    copies.wait()


def edges(pieces):
    return pl.pallas_call(
        edges_kernel,
        out_shape=tuple(jax.ShapeDtypeStruct(s, F32) for s in (ZEDGE, ZEDGE, CORNER, CORNER)),
        in_specs=[ANY] * 8,
        out_specs=(ANY,) * 4,
        scratch_shapes=[
            pltpu.VMEM(TILE, F32),
            pltpu.SemaphoreType.DMA((8,)),
            pltpu.SemaphoreType.DMA((4,)),
        ],
        compiler_params=params(),
        name="edges",
    )(*pieces)


def slab_kernel(*refs):
    pieces, out = refs[:8], refs[8]
    slab, sems, out_sems = refs[9:]
    z, y, x, c = place()
    copies = Copies(sems)
    put_pieces(copies, pieces, lambda h, s: slab.at[h, s])
    copies.wait()
    copies = Copies(out_sems)
    copies.add(slab, out)
    copies.wait()


def slab(pieces):
    return pl.pallas_call(
        slab_kernel,
        out_shape=jax.ShapeDtypeStruct((2, 4, 2, 128, 256), F32),
        in_specs=[ANY] * 8,
        out_specs=ANY,
        scratch_shapes=[
            pltpu.VMEM((2, 4, 2, 128, 256), F32),
            pltpu.SemaphoreType.DMA((8,)),
            pltpu.SemaphoreType.DMA((1,)),
        ],
        compiler_params=params(),
        name="slab",
    )(*pieces)


def by_block(pieces, y):
    order = [pieces[0], pieces[3], pieces[2], pieces[1]]
    stack = jnp.stack(order + order[:3])
    return lax.dynamic_slice_in_dim(stack, (YD - y) % YD, 4, axis=0)


def gathered(share):
    return [share] + [x_turn(share, k) for k in (1, 2, 3)]


def local(estimate, views, axial_taps, lateral_taps, cover):
    z, y, x, c = place()

    half = lax.dynamic_slice_in_dim(estimate, 8 * c, 8, axis=0)
    half = jnp.pad(half, ((0, 0), (8, 8), (0, 0))).reshape(4, 2, 18, 8, 256)

    def est_rows(k):
        return lax.dynamic_slice_in_dim(half, 4 * ((y + k) % YD), 6, axis=2)

    def view_rows(k):
        rows = lax.dynamic_slice_in_dim(views[0].reshape(16, 16, 8, 256), 4 * ((y + k) % YD), 4, axis=1)
        return jnp.transpose(rows, (1, 0, 2, 3)).reshape(4, 2, 4, 2, 8, 256)

    pieces = [est_rows(0)] + [y_turn(est_rows(k), k) for k in (1, 2, 3)]
    mats = matrices(axial_taps, lateral_taps)
    shown = [view_rows(k) for k in range(4)]
    pieces, mats, shown = lax.optimization_barrier((pieces, mats, shown))
    shown = [shown[0]] + [y_turn(shown[k], k) for k in (1, 2, 3)]
    share = [lax.dynamic_index_in_dim(p, x, 0, keepdims=False)[:, 1:5] for p in pieces]
    share = by_block(share, y)
    for step in range(ITERS):
        if step == 0:
            top = lax.select_n((y + 1) % YD, *pieces)
            bottom = lax.select_n(y, *pieces)
            beside = [blk_shift(top, 1, 0), blk_shift(bottom, -1, 0)]
            tile = pieces + [core_swap(piece) for piece in pieces]
            tile += beside + [core_swap(part) for part in beside]
        else:
            pieces = gathered(share)
            pieces = pieces + [core_swap(piece) for piece in pieces]
            rims = [core_step(e, steps) for e, steps in zip(edges(pieces), STEPS)]
            swapped = core_swap(jnp.concatenate([rim.reshape(-1, 8, 256) for rim in rims]))
            tile = pieces + rims + [swapped]
        center, rims = forward(step == 0, mats, tile, shown)
        halos = [blk_shift(e, *d) for e, d in zip(rims, FACES)]
        low, high = halos[0], halos[1]
        strips = [blk_shift(jnp.stack([low[r], high[r]]), 0, dy) for r, dy in ((3, 1), (0, -1))]
        mine, other = backward(cover, mats, center, halos, strips)
        terms = shares(mine, core_swap(other))
        total = terms[0]
        for k in (1, 2, 3):
            total = total + x_turn(terms[k], k)
        share = share * jnp.exp(total)
    share = share.reshape(4, 2, 32, 256)
    parts = [lax.dynamic_index_in_dim(share, (y + k) % YD, 0, keepdims=False) for k in range(4)]
    parts = [parts[0]] + [y_turn(parts[k], k) for k in (1, 2, 3)]
    strip = by_block(parts, y)
    strip = jnp.transpose(strip, (1, 0, 2, 3)).reshape(2, 128, 256)
    pieces = gathered(strip)
    pieces = pieces + [core_swap(piece) for piece in pieces]
    return slab(pieces).reshape(16, 128, 256)


def solution(mesh):
    in_specs = (
        P("blk", None, None),
        P("view", "blk", None, None),
        P("view", None),
        P("view", None, None),
        P("view", None),
    )
    out_specs = P("blk", None, None)
    return jax.shard_map(local, mesh=mesh, in_specs=in_specs, out_specs=out_specs, check_vma=False)
```

```python
import functools

import jax
import jax.numpy as jnp
from jax import lax
from jax.experimental import pallas as pl
from jax.experimental.pallas import tpu as pltpu
from jax.sharding import PartitionSpec as P

RAD = 8
RZ = 16
ITERS = 2
YD = 4
XD = 4
F32 = jnp.float32
BF16 = jnp.bfloat16
NLAT = 2 * RAD + 1
NAX = 2 * RZ + 1

ANY = pl.BlockSpec(memory_space=pl.ANY)
SMEM = pl.BlockSpec(memory_space=pltpu.SMEM)
VMEM = pl.BlockSpec(memory_space=pltpu.VMEM)
STEPS = (((1, 0), (0, 1)), ((-1, 0), (0, -1)), ((1, 1), (1, -1)), ((-1, -1), (-1, 1)))


def params(mebibytes):
    return pltpu.CompilerParams(vmem_limit_bytes=mebibytes * 1024 * 1024)


def blk_shift(value, dz, dy):
    count = lax.axis_size("blk") // YD
    pairs = [
        (z * YD + y, (z + dz) * YD + y + dy)
        for z in range(count)
        for y in range(YD)
        if 0 <= z + dz < count and 0 <= y + dy < YD
    ]
    return lax.ppermute(value, "blk", pairs)


def core_step(value, steps):
    count = lax.axis_size("blk") // YD
    views = lax.axis_size("view")
    pairs = []
    for z in range(count):
        for y in range(YD):
            for v in range(views):
                dz, dy = steps[v % 2]
                if 0 <= z + dz < count and 0 <= y + dy < YD:
                    target = (z + dz) * YD + y + dy
                    pairs.append(((z * YD + y) * views + v, target * views + v))
    return lax.ppermute(value, ("blk", "view"), pairs)


def y_turn(value, k):
    count = lax.axis_size("blk") // YD
    pairs = [(z * YD + y, z * YD + (y + k) % YD) for z in range(count) for y in range(YD)]
    return lax.ppermute(value, "blk", pairs)


def x_turn(value, k):
    pairs = [(2 * x + c, 2 * ((x + k) % XD) + c) for x in range(XD) for c in range(2)]
    return lax.ppermute(value, "view", pairs)


def core_swap(value):
    return lax.ppermute(value, "view", [(i, i ^ 1) for i in range(2 * XD)])


def split(value):
    high = value.astype(BF16)
    return high, (value - high.astype(F32)).astype(BF16)


def mm(a, b):
    return jnp.dot(a, b, preferred_element_type=F32)


def matrices_kernel(axial_taps, lateral_taps, ky, kzh, kzl, kxh, kxl):
    one = jnp.int32(1)
    zero = jnp.int32(0)

    def iota(shape, axis):
        return lax.broadcasted_iota(jnp.int32, shape, axis)

    def fill(shape, offset, tap, count, put):
        taps = [tap(d) for d in range(count)]
        norm = sum(taps[1:], taps[0])

        @pl.loop(0, shape[0] // 16)
        def _(n):
            start = pl.multiple_of(16 * n, 16)
            where = offset((16, shape[1]), start)
            for way in range(2):
                matrix = jnp.zeros((16, shape[1]), F32)
                for d in range(count):
                    matrix = jnp.where(where == (d if way == 0 else count - 1 - d), taps[d], matrix)
                put(way, pl.ds(start, 16), split(matrix / jnp.full((16, shape[1]), norm)))

    def three(depth, out):
        def part(shape):
            col = iota(shape, 1)
            return jnp.where(col >= depth, one, zero) + jnp.where(col >= 2 * depth, one, zero)

        def offset(shape, start):
            return iota(shape, 1) - depth * part(shape) - iota(shape, 0) - start

        def put(way, rows, parts):
            high, low = [value.astype(F32) for value in parts]
            out[way, rows] = jnp.where(part(high.shape) == 1, low, high).astype(BF16)

        return (32, 3 * depth), offset, put

    def wide(shape, start):
        return iota(shape, 0) + start - iota(shape, 1) + RAD

    def put_wide(way, rows, parts):
        kxh[way, rows], kxl[way, rows] = parts

    shape, offset, put = three(32 + 2 * RAD, ky)
    fill(shape, offset, lambda d: lateral_taps[0, 0, d], NLAT, put)
    fill((256, 256), wide, lambda d: lateral_taps[0, 1, d], NLAT, put_wide)

    def deep(shape, start):
        return iota(shape, 1) - iota(shape, 0) - start

    def put_deep(way, rows, parts):
        kzh[way, rows], kzl[way, rows] = parts

    fill((64, 96), deep, lambda d: axial_taps[0, d], NAX, put_deep)


def matrices(axial_taps, lateral_taps):
    ky = jax.ShapeDtypeStruct((2, 32, 144), BF16)
    kz = jax.ShapeDtypeStruct((2, 64, 96), BF16)
    kx = jax.ShapeDtypeStruct((2, 256, 256), BF16)
    return pl.pallas_call(
        matrices_kernel,
        out_shape=(ky, kz, kz, kx, kx),
        in_specs=[SMEM, SMEM],
        out_specs=(VMEM,) * 5,
        compiler_params=params(8),
        name="matrices",
    )(axial_taps, lateral_taps)


def both_halves(ref, group, rows):
    return jnp.concatenate([ref[0, group, rows, :], ref[1, group, rows, :]], axis=1)


def store_halves(ref, group, rows, value):
    ref[0, group, rows, :] = value[:, :128]
    ref[1, group, rows, :] = value[:, 128:]


def three_products(matrix, high, low):
    return mm(matrix, jnp.concatenate([high, high, low], axis=0))


def blur(way, mats, wide, across, inner, outer, ready, finish, done):
    ky, kzh, kzl, kxh, kxl = [m[way] for m in mats]

    def over_rows(b):
        for n in range(16):
            block = wide[b, n // 8, (n // 2) % 4, n % 2].reshape(48, 256)
            rows = three_products(ky, *split(block))
            at = pl.ds(pl.multiple_of(128 * b + 8 * n, 8), 8)
            for q in range(4):
                store_halves(across, q, at, rows[8 * q : 8 * q + 8])

    inner()

    @pl.loop(0, 6)
    def _(n):
        pl.when(n == 4)(outer)
        over_rows(jnp.where(n < 4, n + 1, 5 * (n - 4)))

    ready()

    @pl.loop(0, 8)
    def _(n):
        q = n // 2
        r0 = 4 * (n % 2)
        deep = []
        for r in range(4):
            high, low = split(both_halves(across, q, pl.ds(r0 + r, 96, stride=8)))
            deep.append(mm(kzh, high) + (mm(kzl, high) + mm(kzh, low)))
        high, low = split(jnp.concatenate(deep, axis=0))
        both = mm(high, kxh) + (mm(low, kxh) + mm(high, kxl))
        for r in range(4):
            finish(q, pl.ds(r0 + r, 64, stride=8), both[64 * r : 64 * r + 64])

        @pl.when(r0 > 0)
        def _():
            done(q)


def halo_slot(wide, step):
    dz, dy = step
    b = {1: 0, -1: 5, 0: pl.ds(1, 4)}[dz]
    r = {1: 0, -1: 5, 0: pl.ds(1, 4)}[dy]
    return wide.at[b, :, :, :, r]


def edge_of(tile, step):
    dz, dy = step
    b = {-1: 0, 1: 3, 0: pl.ds(0, 4)}[dz]
    r = {-1: 0, 1: 3, 0: pl.ds(0, 4)}[dy]
    return tile.at[b, :, :, :, r]


def place():
    blk = lax.axis_index("blk")
    view = lax.axis_index("view")
    return blk // YD, blk % YD, view // 2, view % 2


class Copies:
    def __init__(self, sems):
        self.sems = sems
        self.items = []

    def add(self, source, target):
        item = pltpu.make_async_copy(source, target, self.sems.at[len(self.items)])
        item.start()
        self.items.append(item)
        return len(self.items)

    def add_by_core(self, c, pair0, pair1):
        items = [pltpu.make_async_copy(*p, self.sems.at[len(self.items)]) for p in (pair0, pair1)]
        pl.when(c == 0)(items[0].start)
        pl.when(c != 0)(items[1].start)
        self.items.append(items[0])

    def wait(self, first=0, end=None):
        for item in self.items[first:end]:
            item.wait()


TILE = (4, 2, 4, 2, 4, 8, 256)
WIDE = (6, 2, 4, 2, 6, 8, 256)
ZEDGE = (2, 4, 2, 4, 8, 256)
YEDGE = (4, 2, 4, 2, 8, 256)
CORNER = (2, 4, 2, 8, 256)
PART = (4, 2, 4, 8, 256)
RATIO = (4, 4, 2, 4, 2, 8, 256)
RATIO_ZEDGE = (4, 2, 4, 2, 8, 256)
FACES = ((1, 0), (-1, 0), (0, 1), (0, -1))


def grouped(ref, half):
    return ref.at[half].reshape(4, 4, 2, 4, 2, 8, 128)


def put_pieces(copies, pieces, tile):
    z, y, x, c = place()
    for k in range(4):
        s = (x - k + XD) % XD
        for other in range(2):
            half = c if other == 0 else 1 - c
            copies.add(pieces[4 * other + k], tile(half, s))


def forward_kernel(first, *refs):
    inputs = 17 if first else 18
    mats, tile, refs = refs[:5], refs[5:inputs], refs[inputs:]
    shown, center, edges = refs[:4], refs[4], refs[5:9]
    wide, across, views, ratio, sems, group_sems, out_sems = refs[9:]
    z, y, x, c = place()
    copies = Copies(sems)
    middle = wide.at[pl.ds(1, 4)]
    if first:
        for other in range(2):
            half = c if other == 0 else 1 - c
            for k in range(4):
                copies.add(tile[4 * other + k], middle.at[(y - k + YD) % YD, half])
            for n in range(2):
                copies.add(tile[8 + 2 * other + n], wide.at[5 * n, half])
    else:
        pieces, moved, got = tile[:8], tile[8:12], tile[12]
        put_pieces(copies, pieces, lambda h, s: middle.at[:, h, s, :, pl.ds(1, 4)])
        for n, (step0, step1) in enumerate(STEPS):
            shapes = (ZEDGE, YEDGE) if n < 2 else (CORNER, CORNER)
            start, size = (64 * n, 64) if n < 2 else (96 + 16 * n, 16)
            theirs = got.at[pl.ds(start, size)]
            slot0, slot1 = halo_slot(wide, step0), halo_slot(wide, step1)
            copies.add_by_core(c, (moved[n], slot0), (theirs.reshape(*shapes[0]), slot0))
            own = moved[n].reshape(*shapes[1])
            copies.add_by_core(c, (theirs.reshape(*shapes[1]), slot1), (own, slot1))
    count = len(copies.items)
    for k in range(4):
        b = (y - k + YD) % YD
        for half in range(2):
            copies.add(shown[k].at[..., pl.ds(128 * half, 128)], grouped(views, half).at[:, b])

    def finish(group, rows, value):
        store_halves(ratio, group, rows, both_halves(views, group, rows) / value)

    def group_copies(q):
        for half in range(2):
            tile = grouped(ratio, half).at[q]
            lanes = pl.ds(128 * half, 128)
            for n, (source, target) in enumerate(((3, edges[0]), (0, edges[1]), (None, center))):
                source = tile if source is None else tile.at[source]
                yield pltpu.make_async_copy(source, target.at[q, ..., lanes], group_sems.at[q, half, n])

    def done(q):
        for item in group_copies(q):
            item.start()

    blur(
        0,
        mats,
        wide,
        across,
        lambda: copies.wait(0, count),
        lambda: None,
        lambda: copies.wait(count),
        finish,
        done,
    )
    copies = Copies(out_sems)
    for half in range(2):
        tile = grouped(ratio, half)
        lanes = pl.ds(128 * half, 128)
        for n, edge in ((2, tile.at[3]), (3, tile.at[0])):
            copies.add(edge, edges[n].at[..., lanes])
    for q in range(4):
        for item in group_copies(q):
            item.wait()
    copies.wait()


def forward(first, mats, tile, shown):
    shapes = (RATIO, RATIO_ZEDGE, RATIO_ZEDGE, YEDGE, YEDGE)
    got = pl.pallas_call(
        functools.partial(forward_kernel, first),
        out_shape=tuple(jax.ShapeDtypeStruct(s, F32) for s in shapes),
        in_specs=[VMEM] * 5 + [ANY] * (len(tile) + 4),
        out_specs=(ANY,) * 5,
        scratch_shapes=[
            pltpu.VMEM(WIDE, F32),
            pltpu.VMEM((2, 4, 768, 128), F32),
            pltpu.VMEM((2, 4, 512, 128), F32),
            pltpu.VMEM((2, 4, 512, 128), F32),
            pltpu.SemaphoreType.DMA((24,)),
            pltpu.SemaphoreType.DMA((4, 2, 3)),
            pltpu.SemaphoreType.DMA((4,)),
        ],
        compiler_params=params(18),
        name="forward",
    )(*mats, *tile, *shown)
    return got[0], got[1:]


def backward_kernel(cover, *refs):
    mats, center, halos, strips = refs[:5], refs[5], refs[6:10], refs[10:12]
    mine, other = refs[12:14]
    wide, across, logs, sems, out_sems = refs[14:]
    z, y, x, c = place()
    copies = Copies(sems)
    for n in range(2, 4):
        copies.add(halos[n], halo_slot(wide, FACES[n]))
    for q in range(4):
        count = copies.add(center.at[q], wide.at[pl.ds(1, 4), :, :, :, 1 + q])
    for q in range(4):
        for n in range(2):
            copies.add(halos[n].at[q], wide.at[5 * n, :, :, :, 1 + q])
    for n, dy in enumerate((1, -1)):
        for m, dz in enumerate((1, -1)):
            copies.add(strips[n].at[m], halo_slot(wide, (dz, dy)))
    plane = z * 64 + lax.broadcasted_iota(jnp.int32, (64, 256), 0)
    inside = jnp.logical_and(plane >= cover[0, 0], plane < cover[0, 1])

    def finish(group, rows, value):
        store_halves(logs, group, rows, jnp.where(inside, jnp.log(value), jnp.float32(0.0)))

    def group_copies(q):
        for half in range(2):
            tile = grouped(logs, half).at[q]
            lanes = pl.ds(128 * half, 128)
            for n, (core, target) in enumerate(((1 - c, other), (c, mine))):
                target = target.at[:, :, :, q, :, lanes]
                yield pltpu.make_async_copy(tile.at[:, core], target, out_sems.at[q, half, n])

    def done(q):
        for item in group_copies(q):
            item.start()

    blur(
        1,
        mats,
        wide,
        across,
        lambda: copies.wait(0, count),
        lambda: copies.wait(count),
        lambda: None,
        finish,
        done,
    )
    for q in range(4):
        for item in group_copies(q):
            item.wait()


def backward(cover, mats, center, halos, strips):
    half = jax.ShapeDtypeStruct((4,) + PART, F32)
    return pl.pallas_call(
        backward_kernel,
        out_shape=(half, half),
        in_specs=[SMEM] + [VMEM] * 5 + [ANY] * 7,
        out_specs=(ANY, ANY),
        scratch_shapes=[
            pltpu.VMEM(WIDE, F32),
            pltpu.VMEM((2, 4, 768, 128), F32),
            pltpu.VMEM((2, 4, 512, 128), F32),
            pltpu.SemaphoreType.DMA((18,)),
            pltpu.SemaphoreType.DMA((4, 2, 2)),
        ],
        compiler_params=params(16),
        name="backward",
    )(cover, *mats, center, *halos, *strips)


def shares_kernel(mine, got, *outs):
    z, y, x, c = place()
    for k in range(4):
        s = (x + k) % XD

        @pl.loop(0, 4)
        def _(b):
            outs[k][b] = mine[b, s] + got[b, s]


def shares(mine, got):
    part = jax.ShapeDtypeStruct(PART, F32)
    return pl.pallas_call(
        shares_kernel,
        out_shape=(part,) * 4,
        in_specs=[VMEM, VMEM],
        out_specs=(VMEM,) * 4,
        compiler_params=params(8),
        name="shares",
    )(mine, got)


def edges_kernel(*refs):
    pieces, outs = refs[:8], refs[8:12]
    tile, sems, out_sems = refs[12:]
    z, y, x, c = place()
    copies = Copies(sems)
    put_pieces(copies, pieces, lambda h, s: tile.at[:, h, s])
    copies.wait()
    copies = Copies(out_sems)
    for n, (step0, step1) in enumerate(STEPS):
        out1 = outs[n].reshape(*YEDGE) if n < 2 else outs[n]
        copies.add_by_core(c, (edge_of(tile, step0), outs[n]), (edge_of(tile, step1), out1))
    copies.wait()


def edges(pieces):
    return pl.pallas_call(
        edges_kernel,
        out_shape=tuple(jax.ShapeDtypeStruct(s, F32) for s in (ZEDGE, ZEDGE, CORNER, CORNER)),
        in_specs=[ANY] * 8,
        out_specs=(ANY,) * 4,
        scratch_shapes=[
            pltpu.VMEM(TILE, F32),
            pltpu.SemaphoreType.DMA((8,)),
            pltpu.SemaphoreType.DMA((4,)),
        ],
        compiler_params=params(6),
        name="edges",
    )(*pieces)


def slab_kernel(*refs):
    pieces, out = refs[:8], refs[8]
    slab, sems, out_sems = refs[9:]
    z, y, x, c = place()
    copies = Copies(sems)
    put_pieces(copies, pieces, lambda h, s: slab.at[h, s])
    copies.wait()
    copies = Copies(out_sems)
    copies.add(slab, out)
    copies.wait()


def slab(pieces):
    return pl.pallas_call(
        slab_kernel,
        out_shape=jax.ShapeDtypeStruct((2, 4, 2, 128, 256), F32),
        in_specs=[ANY] * 8,
        out_specs=ANY,
        scratch_shapes=[
            pltpu.VMEM((2, 4, 2, 128, 256), F32),
            pltpu.SemaphoreType.DMA((8,)),
            pltpu.SemaphoreType.DMA((1,)),
        ],
        compiler_params=params(6),
        name="slab",
    )(*pieces)


def by_block(pieces, y):
    order = [pieces[0], pieces[3], pieces[2], pieces[1]]
    stack = jnp.stack(order + order[:3])
    return lax.dynamic_slice_in_dim(stack, (YD - y) % YD, 4, axis=0)


def gathered(share):
    return [share] + [x_turn(share, k) for k in (1, 2, 3)]


def local(estimate, views, axial_taps, lateral_taps, cover):
    z, y, x, c = place()

    half = lax.dynamic_slice_in_dim(estimate, 8 * c, 8, axis=0)
    half = jnp.pad(half, ((0, 0), (8, 8), (0, 0))).reshape(4, 2, 18, 8, 256)

    def est_rows(k):
        return lax.dynamic_slice_in_dim(half, 4 * ((y + k) % YD), 6, axis=2)

    def view_rows(k):
        rows = lax.dynamic_slice_in_dim(views[0].reshape(16, 16, 8, 256), 4 * ((y + k) % YD), 4, axis=1)
        return jnp.transpose(rows, (1, 0, 2, 3)).reshape(4, 2, 4, 2, 8, 256)

    pieces = [est_rows(0)] + [y_turn(est_rows(k), k) for k in (1, 2, 3)]
    mats = matrices(axial_taps, lateral_taps)
    shown = [view_rows(k) for k in range(4)]
    pieces, mats, shown = lax.optimization_barrier((pieces, mats, shown))
    shown = [shown[0]] + [y_turn(shown[k], k) for k in (1, 2, 3)]
    share = [lax.dynamic_index_in_dim(p, x, 0, keepdims=False)[:, 1:5] for p in pieces]
    share = by_block(share, y)
    for step in range(ITERS):
        if step == 0:
            top = lax.select_n((y + 1) % YD, *pieces)
            bottom = lax.select_n(y, *pieces)
            beside = [blk_shift(top, 1, 0), blk_shift(bottom, -1, 0)]
            tile = pieces + [core_swap(piece) for piece in pieces]
            tile += beside + [core_swap(part) for part in beside]
        else:
            pieces = gathered(share)
            pieces = pieces + [core_swap(piece) for piece in pieces]
            rims = [core_step(e, steps) for e, steps in zip(edges(pieces), STEPS)]
            swapped = core_swap(jnp.concatenate([rim.reshape(-1, 8, 256) for rim in rims]))
            tile = pieces + rims + [swapped]
        center, rims = forward(step == 0, mats, tile, shown)
        halos = [blk_shift(e, *d) for e, d in zip(rims, FACES)]
        low, high = halos[0], halos[1]
        strips = [blk_shift(jnp.stack([low[r], high[r]]), 0, dy) for r, dy in ((3, 1), (0, -1))]
        mine, other = backward(cover, mats, center, halos, strips)
        terms = shares(mine, core_swap(other))
        total = terms[0]
        for k in (1, 2, 3):
            total = total + x_turn(terms[k], k)
        share = share * jnp.exp(total)
    share = share.reshape(4, 2, 32, 256)
    parts = [lax.dynamic_index_in_dim(share, (y + k) % YD, 0, keepdims=False) for k in range(4)]
    parts = [parts[0]] + [y_turn(parts[k], k) for k in (1, 2, 3)]
    strip = by_block(parts, y)
    strip = jnp.transpose(strip, (1, 0, 2, 3)).reshape(2, 128, 256)
    pieces = gathered(strip)
    pieces = pieces + [core_swap(piece) for piece in pieces]
    return slab(pieces).reshape(16, 128, 256)


def solution(mesh):
    in_specs = (
        P("blk", None, None),
        P("view", "blk", None, None),
        P("view", None),
        P("view", None, None),
        P("view", None),
    )
    out_specs = P("blk", None, None)
    return jax.shard_map(local, mesh=mesh, in_specs=in_specs, out_specs=out_specs, check_vma=False)
```

```python
import functools

import jax
import jax.numpy as jnp
from jax import lax
from jax.experimental import pallas as pl
from jax.experimental.pallas import tpu as pltpu
from jax.sharding import PartitionSpec as P

RAD = 8
RZ = 16
ITERS = 2
YD = 4
XD = 4
F32 = jnp.float32
BF16 = jnp.bfloat16
NLAT = 2 * RAD + 1
NAX = 2 * RZ + 1

ANY = pl.BlockSpec(memory_space=pl.ANY)
SMEM = pl.BlockSpec(memory_space=pltpu.SMEM)
VMEM = pl.BlockSpec(memory_space=pltpu.VMEM)
STEPS = (((1, 0), (0, 1)), ((-1, 0), (0, -1)), ((1, 1), (1, -1)), ((-1, -1), (-1, 1)))


def params(mebibytes):
    return pltpu.CompilerParams(vmem_limit_bytes=mebibytes * 1024 * 1024)


def blk_shift(value, dz, dy):
    count = lax.axis_size("blk") // YD
    pairs = [
        (z * YD + y, (z + dz) * YD + y + dy)
        for z in range(count)
        for y in range(YD)
        if 0 <= z + dz < count and 0 <= y + dy < YD
    ]
    return lax.ppermute(value, "blk", pairs)


def core_step(value, steps):
    count = lax.axis_size("blk") // YD
    views = lax.axis_size("view")
    pairs = []
    for z in range(count):
        for y in range(YD):
            for v in range(views):
                dz, dy = steps[v % 2]
                if 0 <= z + dz < count and 0 <= y + dy < YD:
                    target = (z + dz) * YD + y + dy
                    pairs.append(((z * YD + y) * views + v, target * views + v))
    return lax.ppermute(value, ("blk", "view"), pairs)


def y_turn(value, k):
    count = lax.axis_size("blk") // YD
    pairs = [(z * YD + y, z * YD + (y + k) % YD) for z in range(count) for y in range(YD)]
    return lax.ppermute(value, "blk", pairs)


def x_turn(value, k):
    pairs = [(2 * x + c, 2 * ((x + k) % XD) + c) for x in range(XD) for c in range(2)]
    return lax.ppermute(value, "view", pairs)


def core_swap(value):
    return lax.ppermute(value, "view", [(i, i ^ 1) for i in range(2 * XD)])


def split(value):
    high = value.astype(BF16)
    return high, (value - high.astype(F32)).astype(BF16)


def mm(a, b):
    return jnp.dot(a, b, preferred_element_type=F32)


def matrices_kernel(axial_taps, lateral_taps, ky, kzh, kzl, kxh, kxl):
    one = jnp.int32(1)
    zero = jnp.int32(0)

    def iota(shape, axis):
        return lax.broadcasted_iota(jnp.int32, shape, axis)

    def fill(shape, offset, tap, count, put):
        taps = [tap(d) for d in range(count)]
        norm = sum(taps[1:], taps[0])

        @pl.loop(0, shape[0] // 16)
        def _(n):
            start = pl.multiple_of(16 * n, 16)
            where = offset((16, shape[1]), start)
            for way in range(2):
                matrix = jnp.zeros((16, shape[1]), F32)
                for d in range(count):
                    matrix = jnp.where(where == (d if way == 0 else count - 1 - d), taps[d], matrix)
                put(way, pl.ds(start, 16), split(matrix / jnp.full((16, shape[1]), norm)))

    def three(depth, out):
        def part(shape):
            col = iota(shape, 1)
            return jnp.where(col >= depth, one, zero) + jnp.where(col >= 2 * depth, one, zero)

        def offset(shape, start):
            return iota(shape, 1) - depth * part(shape) - iota(shape, 0) - start

        def put(way, rows, parts):
            high, low = [value.astype(F32) for value in parts]
            out[way, rows] = jnp.where(part(high.shape) == 1, low, high).astype(BF16)

        return (32, 3 * depth), offset, put

    def wide(shape, start):
        return iota(shape, 0) + start - iota(shape, 1) + RAD

    def put_wide(way, rows, parts):
        kxh[way, rows], kxl[way, rows] = parts

    shape, offset, put = three(32 + 2 * RAD, ky)
    fill(shape, offset, lambda d: lateral_taps[0, 0, d], NLAT, put)
    fill((256, 256), wide, lambda d: lateral_taps[0, 1, d], NLAT, put_wide)

    def deep(shape, start):
        return iota(shape, 1) - iota(shape, 0) - start

    def put_deep(way, rows, parts):
        kzh[way, rows], kzl[way, rows] = parts

    fill((64, 96), deep, lambda d: axial_taps[0, d], NAX, put_deep)


def matrices(axial_taps, lateral_taps):
    ky = jax.ShapeDtypeStruct((2, 32, 144), BF16)
    kz = jax.ShapeDtypeStruct((2, 64, 96), BF16)
    kx = jax.ShapeDtypeStruct((2, 256, 256), BF16)
    return pl.pallas_call(
        matrices_kernel,
        out_shape=(ky, kz, kz, kx, kx),
        in_specs=[SMEM, SMEM],
        out_specs=(VMEM,) * 5,
        compiler_params=params(8),
        name="matrices",
    )(axial_taps, lateral_taps)


def both_halves(ref, group, rows):
    return jnp.concatenate([ref[0, group, rows, :], ref[1, group, rows, :]], axis=1)


def store_halves(ref, group, rows, value):
    ref[0, group, rows, :] = value[:, :128]
    ref[1, group, rows, :] = value[:, 128:]


def three_products(matrix, high, low):
    return mm(matrix, jnp.concatenate([high, high, low], axis=0))


def blur(way, mats, wide, across, inner, outer, ready, finish, done):
    ky, kzh, kzl, kxh, kxl = [m[way] for m in mats]

    def over_rows(b):
        for n in range(16):
            block = wide[b, n // 8, (n // 2) % 4, n % 2].reshape(48, 256)
            rows = three_products(ky, *split(block))
            at = pl.ds(pl.multiple_of(128 * b + 8 * n, 8), 8)
            for q in range(4):
                store_halves(across, q, at, rows[8 * q : 8 * q + 8])

    inner()

    @pl.loop(0, 6)
    def _(n):
        pl.when(n == 4)(outer)
        over_rows(jnp.where(n < 4, n + 1, 5 * (n - 4)))

    ready()

    @pl.loop(0, 8)
    def _(n):
        q = n // 2
        r0 = 4 * (n % 2)
        deep = []
        for r in range(4):
            high, low = split(both_halves(across, q, pl.ds(r0 + r, 96, stride=8)))
            deep.append(mm(kzh, high) + (mm(kzl, high) + mm(kzh, low)))
        high, low = split(jnp.concatenate(deep, axis=0))
        both = mm(high, kxh) + (mm(low, kxh) + mm(high, kxl))
        for r in range(4):
            finish(q, pl.ds(r0 + r, 64, stride=8), both[64 * r : 64 * r + 64])

        @pl.when(r0 > 0)
        def _():
            done(q)


def halo_slot(wide, step):
    dz, dy = step
    b = {1: 0, -1: 5, 0: pl.ds(1, 4)}[dz]
    r = {1: 0, -1: 5, 0: pl.ds(1, 4)}[dy]
    return wide.at[b, :, :, :, r]


def edge_of(tile, step):
    dz, dy = step
    b = {-1: 0, 1: 3, 0: pl.ds(0, 4)}[dz]
    r = {-1: 0, 1: 3, 0: pl.ds(0, 4)}[dy]
    return tile.at[b, :, :, :, r]


def place():
    blk = lax.axis_index("blk")
    view = lax.axis_index("view")
    return blk // YD, blk % YD, view // 2, view % 2


class Copies:
    def __init__(self, sems):
        self.sems = sems
        self.items = []

    def add(self, source, target):
        item = pltpu.make_async_copy(source, target, self.sems.at[len(self.items)])
        item.start()
        self.items.append(item)
        return len(self.items)

    def add_by_core(self, c, pair0, pair1):
        items = [pltpu.make_async_copy(*p, self.sems.at[len(self.items)]) for p in (pair0, pair1)]
        pl.when(c == 0)(items[0].start)
        pl.when(c != 0)(items[1].start)
        self.items.append(items[0])

    def wait(self, first=0, end=None):
        for item in self.items[first:end]:
            item.wait()


TILE = (4, 2, 4, 2, 4, 8, 256)
WIDE = (6, 2, 4, 2, 6, 8, 256)
ZEDGE = (2, 4, 2, 4, 8, 256)
YEDGE = (4, 2, 4, 2, 8, 256)
CORNER = (2, 4, 2, 8, 256)
PART = (4, 2, 4, 8, 256)
RATIO = (4, 4, 2, 4, 2, 8, 256)
RATIO_ZEDGE = (4, 2, 4, 2, 8, 256)
FACES = ((1, 0), (-1, 0), (0, 1), (0, -1))


def grouped(ref, half):
    return ref.at[half].reshape(4, 4, 2, 4, 2, 8, 128)


def put_pieces(copies, pieces, tile):
    z, y, x, c = place()
    for k in range(4):
        s = (x - k + XD) % XD
        for other in range(2):
            half = c if other == 0 else 1 - c
            copies.add(pieces[4 * other + k], tile(half, s))


def forward_kernel(first, *refs):
    inputs = 17 if first else 18
    mats, tile, refs = refs[:5], refs[5:inputs], refs[inputs:]
    shown, center, edges = refs[:4], refs[4], refs[5:9]
    wide, across, views, ratio, sems, group_sems, out_sems = refs[9:]
    z, y, x, c = place()
    copies = Copies(sems)
    middle = wide.at[pl.ds(1, 4)]
    if first:
        for other in range(2):
            half = c if other == 0 else 1 - c
            for k in range(4):
                copies.add(tile[4 * other + k], middle.at[(y - k + YD) % YD, half])
            for n in range(2):
                copies.add(tile[8 + 2 * other + n], wide.at[5 * n, half])
    else:
        pieces, moved, got = tile[:8], tile[8:12], tile[12]
        put_pieces(copies, pieces, lambda h, s: middle.at[:, h, s, :, pl.ds(1, 4)])
        for n, (step0, step1) in enumerate(STEPS):
            shapes = (ZEDGE, YEDGE) if n < 2 else (CORNER, CORNER)
            start, size = (64 * n, 64) if n < 2 else (96 + 16 * n, 16)
            theirs = got.at[pl.ds(start, size)]
            slot0, slot1 = halo_slot(wide, step0), halo_slot(wide, step1)
            copies.add_by_core(c, (moved[n], slot0), (theirs.reshape(*shapes[0]), slot0))
            own = moved[n].reshape(*shapes[1])
            copies.add_by_core(c, (theirs.reshape(*shapes[1]), slot1), (own, slot1))
    count = len(copies.items)
    for k in range(4):
        b = (y - k + YD) % YD
        for half in range(2):
            copies.add(shown[k].at[..., pl.ds(128 * half, 128)], grouped(views, half).at[:, b])

    def finish(group, rows, value):
        store_halves(ratio, group, rows, both_halves(views, group, rows) / value)

    def group_copies(q):
        for half in range(2):
            tile = grouped(ratio, half).at[q]
            lanes = pl.ds(128 * half, 128)
            for n, (source, target) in enumerate(((3, edges[0]), (0, edges[1]), (None, center))):
                source = tile if source is None else tile.at[source]
                yield pltpu.make_async_copy(source, target.at[q, ..., lanes], group_sems.at[q, half, n])

    def done(q):
        for item in group_copies(q):
            item.start()

    blur(
        0,
        mats,
        wide,
        across,
        lambda: copies.wait(0, count),
        lambda: None,
        lambda: copies.wait(count),
        finish,
        done,
    )
    copies = Copies(out_sems)
    for half in range(2):
        tile = grouped(ratio, half)
        lanes = pl.ds(128 * half, 128)
        for n, edge in ((2, tile.at[3]), (3, tile.at[0])):
            copies.add(edge, edges[n].at[..., lanes])
    for q in range(4):
        for item in group_copies(q):
            item.wait()
    copies.wait()


def forward(first, mats, tile, shown):
    shapes = (RATIO, RATIO_ZEDGE, RATIO_ZEDGE, YEDGE, YEDGE)
    got = pl.pallas_call(
        functools.partial(forward_kernel, first),
        out_shape=tuple(jax.ShapeDtypeStruct(s, F32) for s in shapes),
        in_specs=[VMEM] * 5 + [ANY] * (len(tile) + 4),
        out_specs=(ANY,) * 5,
        scratch_shapes=[
            pltpu.VMEM(WIDE, F32),
            pltpu.VMEM((2, 4, 768, 128), F32),
            pltpu.VMEM((2, 4, 512, 128), F32),
            pltpu.VMEM((2, 4, 512, 128), F32),
            pltpu.SemaphoreType.DMA((24,)),
            pltpu.SemaphoreType.DMA((4, 2, 3)),
            pltpu.SemaphoreType.DMA((4,)),
        ],
        compiler_params=params(18),
        name="forward",
    )(*mats, *tile, *shown)
    return got[0], got[1:]


def backward_kernel(cover, *refs):
    mats, center, halos, strips = refs[:5], refs[5], refs[6:10], refs[10:12]
    mine, other = refs[12:14]
    wide, across, logs, sems, out_sems = refs[14:]
    z, y, x, c = place()
    copies = Copies(sems)
    for n in range(2, 4):
        copies.add(halos[n], halo_slot(wide, FACES[n]))
    for q in range(4):
        count = copies.add(center.at[q], wide.at[pl.ds(1, 4), :, :, :, 1 + q])
    for q in range(4):
        for n in range(2):
            copies.add(halos[n].at[q], wide.at[5 * n, :, :, :, 1 + q])
    for n, dy in enumerate((1, -1)):
        for m, dz in enumerate((1, -1)):
            copies.add(strips[n].at[m], halo_slot(wide, (dz, dy)))
    plane = z * 64 + lax.broadcasted_iota(jnp.int32, (64, 256), 0)
    inside = jnp.logical_and(plane >= cover[0, 0], plane < cover[0, 1])

    def finish(group, rows, value):
        store_halves(logs, group, rows, jnp.where(inside, jnp.log(value), jnp.float32(0.0)))

    def group_copies(q):
        for half in range(2):
            tile = grouped(logs, half).at[q]
            lanes = pl.ds(128 * half, 128)
            for n, (core, target) in enumerate(((1 - c, other), (c, mine))):
                target = target.at[:, :, :, q, :, lanes]
                yield pltpu.make_async_copy(tile.at[:, core], target, out_sems.at[q, half, n])

    def done(q):
        for item in group_copies(q):
            item.start()

    blur(
        1,
        mats,
        wide,
        across,
        lambda: copies.wait(0, count),
        lambda: copies.wait(count),
        lambda: None,
        finish,
        done,
    )
    for q in range(4):
        for item in group_copies(q):
            item.wait()


def backward(cover, mats, center, halos, strips):
    half = jax.ShapeDtypeStruct((4,) + PART, F32)
    return pl.pallas_call(
        backward_kernel,
        out_shape=(half, half),
        in_specs=[SMEM] + [VMEM] * 5 + [ANY] * 7,
        out_specs=(ANY, ANY),
        scratch_shapes=[
            pltpu.VMEM(WIDE, F32),
            pltpu.VMEM((2, 4, 768, 128), F32),
            pltpu.VMEM((2, 4, 512, 128), F32),
            pltpu.SemaphoreType.DMA((18,)),
            pltpu.SemaphoreType.DMA((4, 2, 2)),
        ],
        compiler_params=params(16),
        name="backward",
    )(cover, *mats, center, *halos, *strips)


def shares_kernel(mine, got, *outs):
    z, y, x, c = place()
    for k in range(4):
        s = (x + k) % XD

        @pl.loop(0, 4)
        def _(b):
            outs[k][b] = mine[b, s] + got[b, s]


def shares(mine, got):
    part = jax.ShapeDtypeStruct(PART, F32)
    return pl.pallas_call(
        shares_kernel,
        out_shape=(part,) * 4,
        in_specs=[VMEM, VMEM],
        out_specs=(VMEM,) * 4,
        compiler_params=params(8),
        name="shares",
    )(mine, got)


def edges_kernel(*refs):
    pieces, outs = refs[:8], refs[8:12]
    tile, sems, out_sems = refs[12:]
    z, y, x, c = place()
    copies = Copies(sems)
    put_pieces(copies, pieces, lambda h, s: tile.at[:, h, s])
    copies.wait()
    copies = Copies(out_sems)
    for n, (step0, step1) in enumerate(STEPS):
        out1 = outs[n].reshape(*YEDGE) if n < 2 else outs[n]
        copies.add_by_core(c, (edge_of(tile, step0), outs[n]), (edge_of(tile, step1), out1))
    copies.wait()


def edges(pieces):
    return pl.pallas_call(
        edges_kernel,
        out_shape=tuple(jax.ShapeDtypeStruct(s, F32) for s in (ZEDGE, ZEDGE, CORNER, CORNER)),
        in_specs=[ANY] * 8,
        out_specs=(ANY,) * 4,
        scratch_shapes=[
            pltpu.VMEM(TILE, F32),
            pltpu.SemaphoreType.DMA((8,)),
            pltpu.SemaphoreType.DMA((4,)),
        ],
        compiler_params=params(6),
        name="edges",
    )(*pieces)


def slab_kernel(*refs):
    pieces, out = refs[:8], refs[8]
    slab, sems, out_sems = refs[9:]
    z, y, x, c = place()
    copies = Copies(sems)
    put_pieces(copies, pieces, lambda h, s: slab.at[h, s])
    copies.wait()
    copies = Copies(out_sems)
    copies.add(slab, out)
    copies.wait()


def slab(pieces):
    return pl.pallas_call(
        slab_kernel,
        out_shape=jax.ShapeDtypeStruct((2, 4, 2, 128, 256), F32),
        in_specs=[ANY] * 8,
        out_specs=ANY,
        scratch_shapes=[
            pltpu.VMEM((2, 4, 2, 128, 256), F32),
            pltpu.SemaphoreType.DMA((8,)),
            pltpu.SemaphoreType.DMA((1,)),
        ],
        compiler_params=params(6),
        name="slab",
    )(*pieces)


def by_block(pieces, y):
    order = [pieces[0], pieces[3], pieces[2], pieces[1]]
    stack = jnp.stack(order + order[:3])
    return lax.dynamic_slice_in_dim(stack, (YD - y) % YD, 4, axis=0)


def gathered(share):
    return [share] + [x_turn(share, k) for k in (1, 2, 3)]


def local(estimate, views, axial_taps, lateral_taps, cover):
    z, y, x, c = place()

    half = lax.dynamic_slice_in_dim(estimate, 8 * c, 8, axis=0)
    half = jnp.pad(half, ((0, 0), (8, 8), (0, 0))).reshape(4, 2, 18, 8, 256)

    def est_rows(k):
        return lax.dynamic_slice_in_dim(half, 4 * ((y + k) % YD), 6, axis=2)

    def view_rows(k):
        rows = lax.dynamic_slice_in_dim(views[0].reshape(16, 16, 8, 256), 4 * ((y + k) % YD), 4, axis=1)
        return jnp.transpose(rows, (1, 0, 2, 3)).reshape(4, 2, 4, 2, 8, 256)

    pieces = [est_rows(0)] + [y_turn(est_rows(k), k) for k in (1, 2, 3)]
    mats = matrices(axial_taps, lateral_taps)
    shown = [view_rows(k) for k in range(4)]
    pieces, mats = lax.optimization_barrier((pieces, mats))
    shown = [shown[0]] + [y_turn(shown[k], k) for k in (1, 2, 3)]
    share = [lax.dynamic_index_in_dim(p, x, 0, keepdims=False)[:, 1:5] for p in pieces]
    share = by_block(share, y)
    for step in range(ITERS):
        if step == 0:
            top = lax.select_n((y + 1) % YD, *pieces)
            bottom = lax.select_n(y, *pieces)
            beside = [blk_shift(top, 1, 0), blk_shift(bottom, -1, 0)]
            tile = pieces + [core_swap(piece) for piece in pieces]
            beside, shown = lax.optimization_barrier((beside, shown))
            tile += beside + [core_swap(part) for part in beside]
        else:
            pieces = gathered(share)
            pieces = pieces + [core_swap(piece) for piece in pieces]
            rims = [core_step(e, steps) for e, steps in zip(edges(pieces), STEPS)]
            swapped = core_swap(jnp.concatenate([rim.reshape(-1, 8, 256) for rim in rims]))
            tile = pieces + rims + [swapped]
        center, rims = forward(step == 0, mats, tile, shown)
        halos = [blk_shift(e, *d) for e, d in zip(rims, FACES)]
        low, high = halos[0], halos[1]
        strips = [blk_shift(jnp.stack([low[r], high[r]]), 0, dy) for r, dy in ((3, 1), (0, -1))]
        mine, other = backward(cover, mats, center, halos, strips)
        terms = shares(mine, core_swap(other))
        total = terms[0]
        for k in (1, 2, 3):
            total = total + x_turn(terms[k], k)
        share = share * jnp.exp(total)
    share = share.reshape(4, 2, 32, 256)
    parts = [lax.dynamic_index_in_dim(share, (y + k) % YD, 0, keepdims=False) for k in range(4)]
    parts = [parts[0]] + [y_turn(parts[k], k) for k in (1, 2, 3)]
    strip = by_block(parts, y)
    strip = jnp.transpose(strip, (1, 0, 2, 3)).reshape(2, 128, 256)
    pieces = gathered(strip)
    pieces = pieces + [core_swap(piece) for piece in pieces]
    return slab(pieces).reshape(16, 128, 256)


def solution(mesh):
    in_specs = (
        P("blk", None, None),
        P("view", "blk", None, None),
        P("view", None),
        P("view", None, None),
        P("view", None),
    )
    out_specs = P("blk", None, None)
    return jax.shard_map(local, mesh=mesh, in_specs=in_specs, out_specs=out_specs, check_vma=False)
```

```python
import functools

import jax
import jax.numpy as jnp
from jax import lax
from jax.experimental import pallas as pl
from jax.experimental.pallas import tpu as pltpu
from jax.sharding import PartitionSpec as P

RAD = 8
RZ = 16
ITERS = 2
YD = 4
XD = 4
F32 = jnp.float32
BF16 = jnp.bfloat16
NLAT = 2 * RAD + 1
NAX = 2 * RZ + 1

ANY = pl.BlockSpec(memory_space=pl.ANY)
SMEM = pl.BlockSpec(memory_space=pltpu.SMEM)
VMEM = pl.BlockSpec(memory_space=pltpu.VMEM)
STEPS = (((1, 0), (0, 1)), ((-1, 0), (0, -1)), ((1, 1), (1, -1)), ((-1, -1), (-1, 1)))


def params(mebibytes):
    return pltpu.CompilerParams(vmem_limit_bytes=mebibytes * 1024 * 1024)


def blk_shift(value, dz, dy):
    count = lax.axis_size("blk") // YD
    pairs = [
        (z * YD + y, (z + dz) * YD + y + dy)
        for z in range(count)
        for y in range(YD)
        if 0 <= z + dz < count and 0 <= y + dy < YD
    ]
    return lax.ppermute(value, "blk", pairs)


def core_step(value, steps):
    count = lax.axis_size("blk") // YD
    views = lax.axis_size("view")
    pairs = []
    for z in range(count):
        for y in range(YD):
            for v in range(views):
                dz, dy = steps[v % 2]
                if 0 <= z + dz < count and 0 <= y + dy < YD:
                    target = (z + dz) * YD + y + dy
                    pairs.append(((z * YD + y) * views + v, target * views + v))
    return lax.ppermute(value, ("blk", "view"), pairs)


def y_turn(value, k):
    count = lax.axis_size("blk") // YD
    pairs = [(z * YD + y, z * YD + (y + k) % YD) for z in range(count) for y in range(YD)]
    return lax.ppermute(value, "blk", pairs)


def x_turn(value, k):
    pairs = [(2 * x + c, 2 * ((x + k) % XD) + c) for x in range(XD) for c in range(2)]
    return lax.ppermute(value, "view", pairs)


def core_swap(value):
    return lax.ppermute(value, "view", [(i, i ^ 1) for i in range(2 * XD)])


def split(value):
    high = value.astype(BF16)
    return high, (value - high.astype(F32)).astype(BF16)


def mm(a, b):
    return jnp.dot(a, b, preferred_element_type=F32)


def matrices_kernel(axial_taps, lateral_taps, ky, kzh, kzl, kxh, kxl):
    one = jnp.int32(1)
    zero = jnp.int32(0)

    def iota(shape, axis):
        return lax.broadcasted_iota(jnp.int32, shape, axis)

    def fill(shape, offset, tap, count, put):
        taps = [tap(d) for d in range(count)]
        norm = sum(taps[1:], taps[0])

        @pl.loop(0, shape[0] // 16)
        def _(n):
            start = pl.multiple_of(16 * n, 16)
            where = offset((16, shape[1]), start)
            for way in range(2):
                matrix = jnp.zeros((16, shape[1]), F32)
                for d in range(count):
                    matrix = jnp.where(where == (d if way == 0 else count - 1 - d), taps[d], matrix)
                put(way, pl.ds(start, 16), split(matrix / jnp.full((16, shape[1]), norm)))

    def three(depth, out):
        def part(shape):
            col = iota(shape, 1)
            return jnp.where(col >= depth, one, zero) + jnp.where(col >= 2 * depth, one, zero)

        def offset(shape, start):
            return iota(shape, 1) - depth * part(shape) - iota(shape, 0) - start

        def put(way, rows, parts):
            high, low = [value.astype(F32) for value in parts]
            out[way, rows] = jnp.where(part(high.shape) == 1, low, high).astype(BF16)

        return (32, 3 * depth), offset, put

    def wide(shape, start):
        return iota(shape, 0) + start - iota(shape, 1) + RAD

    def put_wide(way, rows, parts):
        kxh[way, rows], kxl[way, rows] = parts

    shape, offset, put = three(32 + 2 * RAD, ky)
    fill(shape, offset, lambda d: lateral_taps[0, 0, d], NLAT, put)
    fill((256, 256), wide, lambda d: lateral_taps[0, 1, d], NLAT, put_wide)

    def deep(shape, start):
        return iota(shape, 1) - iota(shape, 0) - start

    def put_deep(way, rows, parts):
        kzh[way, rows], kzl[way, rows] = parts

    fill((64, 96), deep, lambda d: axial_taps[0, d], NAX, put_deep)


def matrices(axial_taps, lateral_taps):
    ky = jax.ShapeDtypeStruct((2, 32, 144), BF16)
    kz = jax.ShapeDtypeStruct((2, 64, 96), BF16)
    kx = jax.ShapeDtypeStruct((2, 256, 256), BF16)
    return pl.pallas_call(
        matrices_kernel,
        out_shape=(ky, kz, kz, kx, kx),
        in_specs=[SMEM, SMEM],
        out_specs=(VMEM,) * 5,
        compiler_params=params(8),
        name="matrices",
    )(axial_taps, lateral_taps)


def both_halves(ref, group, rows):
    return jnp.concatenate([ref[0, group, rows, :], ref[1, group, rows, :]], axis=1)


def store_halves(ref, group, rows, value):
    ref[0, group, rows, :] = value[:, :128]
    ref[1, group, rows, :] = value[:, 128:]


def three_products(matrix, high, low):
    return mm(matrix, jnp.concatenate([high, high, low], axis=0))


def blur(way, mats, wide, across, inner, outer, ready, finish, done):
    ky, kzh, kzl, kxh, kxl = [m[way] for m in mats]

    def over_rows(b):
        for n in range(16):
            block = wide[b, n // 8, (n // 2) % 4, n % 2].reshape(48, 256)
            rows = three_products(ky, *split(block))
            at = pl.ds(pl.multiple_of(128 * b + 8 * n, 8), 8)
            for q in range(4):
                store_halves(across, q, at, rows[8 * q : 8 * q + 8])

    inner()

    @pl.loop(0, 6)
    def _(n):
        pl.when(n == 4)(outer)
        over_rows(jnp.where(n < 4, n + 1, 5 * (n - 4)))

    ready()

    @pl.loop(0, 8)
    def _(n):
        q = n // 2
        r0 = 4 * (n % 2)
        deep = []
        for r in range(4):
            high, low = split(both_halves(across, q, pl.ds(r0 + r, 96, stride=8)))
            deep.append(mm(kzh, high) + (mm(kzl, high) + mm(kzh, low)))
        high, low = split(jnp.concatenate(deep, axis=0))
        both = mm(high, kxh) + (mm(low, kxh) + mm(high, kxl))
        for r in range(4):
            finish(q, pl.ds(r0 + r, 64, stride=8), both[64 * r : 64 * r + 64])

        @pl.when(r0 > 0)
        def _():
            done(q)


def halo_slot(wide, step):
    dz, dy = step
    b = {1: 0, -1: 5, 0: pl.ds(1, 4)}[dz]
    r = {1: 0, -1: 5, 0: pl.ds(1, 4)}[dy]
    return wide.at[b, :, :, :, r]


def edge_of(tile, step):
    dz, dy = step
    b = {-1: 0, 1: 3, 0: pl.ds(0, 4)}[dz]
    r = {-1: 0, 1: 3, 0: pl.ds(0, 4)}[dy]
    return tile.at[b, :, :, :, r]


def place():
    blk = lax.axis_index("blk")
    view = lax.axis_index("view")
    return blk // YD, blk % YD, view // 2, view % 2


class Copies:
    def __init__(self, sems):
        self.sems = sems
        self.items = []

    def add(self, source, target):
        item = pltpu.make_async_copy(source, target, self.sems.at[len(self.items)])
        item.start()
        self.items.append(item)
        return len(self.items)

    def add_by_core(self, c, pair0, pair1):
        items = [pltpu.make_async_copy(*p, self.sems.at[len(self.items)]) for p in (pair0, pair1)]
        pl.when(c == 0)(items[0].start)
        pl.when(c != 0)(items[1].start)
        self.items.append(items[0])

    def wait(self, first=0, end=None):
        for item in self.items[first:end]:
            item.wait()


TILE = (4, 2, 4, 2, 4, 8, 256)
WIDE = (6, 2, 4, 2, 6, 8, 256)
ZEDGE = (2, 4, 2, 4, 8, 256)
YEDGE = (4, 2, 4, 2, 8, 256)
CORNER = (2, 4, 2, 8, 256)
PART = (4, 2, 4, 8, 256)
RATIO = (4, 4, 2, 4, 2, 8, 256)
RATIO_ZEDGE = (4, 2, 4, 2, 8, 256)
FACES = ((1, 0), (-1, 0), (0, 1), (0, -1))


def grouped(ref, half):
    return ref.at[half].reshape(4, 4, 2, 4, 2, 8, 128)


def put_pieces(copies, pieces, tile):
    z, y, x, c = place()
    for k in range(4):
        s = (x - k + XD) % XD
        for other in range(2):
            half = c if other == 0 else 1 - c
            copies.add(pieces[4 * other + k], tile(half, s))


def forward_kernel(first, *refs):
    inputs = 17 if first else 18
    mats, tile, refs = refs[:5], refs[5:inputs], refs[inputs:]
    shown, center, edges = refs[:4], refs[4], refs[5:9]
    wide, across, views, ratio, sems, group_sems, out_sems = refs[9:]
    z, y, x, c = place()
    copies = Copies(sems)
    middle = wide.at[pl.ds(1, 4)]
    if first:
        for other in range(2):
            half = c if other == 0 else 1 - c
            for k in range(4):
                copies.add(tile[4 * other + k], middle.at[(y - k + YD) % YD, half])
            for n in range(2):
                copies.add(tile[8 + 2 * other + n], wide.at[5 * n, half])
    else:
        pieces, moved, got = tile[:8], tile[8:12], tile[12]
        put_pieces(copies, pieces, lambda h, s: middle.at[:, h, s, :, pl.ds(1, 4)])
        for n, (step0, step1) in enumerate(STEPS):
            shapes = (ZEDGE, YEDGE) if n < 2 else (CORNER, CORNER)
            start, size = (64 * n, 64) if n < 2 else (96 + 16 * n, 16)
            theirs = got.at[pl.ds(start, size)]
            slot0, slot1 = halo_slot(wide, step0), halo_slot(wide, step1)
            copies.add_by_core(c, (moved[n], slot0), (theirs.reshape(*shapes[0]), slot0))
            own = moved[n].reshape(*shapes[1])
            copies.add_by_core(c, (theirs.reshape(*shapes[1]), slot1), (own, slot1))
    count = len(copies.items)
    for k in range(4):
        b = (y - k + YD) % YD
        for half in range(2):
            copies.add(shown[k].at[..., pl.ds(128 * half, 128)], grouped(views, half).at[:, b])

    def finish(group, rows, value):
        store_halves(ratio, group, rows, both_halves(views, group, rows) / value)

    def group_copies(q):
        for half in range(2):
            tile = grouped(ratio, half).at[q]
            lanes = pl.ds(128 * half, 128)
            for n, (source, target) in enumerate(((3, edges[0]), (0, edges[1]), (None, center))):
                source = tile if source is None else tile.at[source]
                yield pltpu.make_async_copy(source, target.at[q, ..., lanes], group_sems.at[q, half, n])

    def done(q):
        for item in group_copies(q):
            item.start()

    blur(
        0,
        mats,
        wide,
        across,
        lambda: copies.wait(0, count),
        lambda: None,
        lambda: copies.wait(count),
        finish,
        done,
    )
    copies = Copies(out_sems)
    for half in range(2):
        tile = grouped(ratio, half)
        lanes = pl.ds(128 * half, 128)
        for n, edge in ((2, tile.at[3]), (3, tile.at[0])):
            copies.add(edge, edges[n].at[..., lanes])
    for q in range(4):
        for item in group_copies(q):
            item.wait()
    copies.wait()


def forward(first, mats, tile, shown):
    shapes = (RATIO, RATIO_ZEDGE, RATIO_ZEDGE, YEDGE, YEDGE)
    got = pl.pallas_call(
        functools.partial(forward_kernel, first),
        out_shape=tuple(jax.ShapeDtypeStruct(s, F32) for s in shapes),
        in_specs=[VMEM] * 5 + [ANY] * (len(tile) + 4),
        out_specs=(ANY,) * 5,
        scratch_shapes=[
            pltpu.VMEM(WIDE, F32),
            pltpu.VMEM((2, 4, 768, 128), F32),
            pltpu.VMEM((2, 4, 512, 128), F32),
            pltpu.VMEM((2, 4, 512, 128), F32),
            pltpu.SemaphoreType.DMA((24,)),
            pltpu.SemaphoreType.DMA((4, 2, 3)),
            pltpu.SemaphoreType.DMA((4,)),
        ],
        compiler_params=params(18),
        name="forward",
    )(*mats, *tile, *shown)
    return got[0], got[1:]


def backward_kernel(cover, *refs):
    mats, center, halos, strips = refs[:5], refs[5], refs[6:10], refs[10:12]
    mine, other = refs[12:14]
    wide, across, logs, sems, out_sems = refs[14:]
    z, y, x, c = place()
    copies = Copies(sems)
    for n in range(2, 4):
        copies.add(halos[n], halo_slot(wide, FACES[n]))
    for q in range(4):
        count = copies.add(center.at[q], wide.at[pl.ds(1, 4), :, :, :, 1 + q])
    for q in range(4):
        for n in range(2):
            copies.add(halos[n].at[q], wide.at[5 * n, :, :, :, 1 + q])
    for n, dy in enumerate((1, -1)):
        for m, dz in enumerate((1, -1)):
            copies.add(strips[n].at[m], halo_slot(wide, (dz, dy)))
    plane = z * 64 + lax.broadcasted_iota(jnp.int32, (64, 256), 0)
    inside = jnp.logical_and(plane >= cover[0, 0], plane < cover[0, 1])

    def finish(group, rows, value):
        store_halves(logs, group, rows, jnp.where(inside, jnp.log(value), jnp.float32(0.0)))

    def group_copies(q):
        for half in range(2):
            tile = grouped(logs, half).at[q]
            lanes = pl.ds(128 * half, 128)
            for n, (core, target) in enumerate(((1 - c, other), (c, mine))):
                target = target.at[:, :, :, q, :, lanes]
                yield pltpu.make_async_copy(tile.at[:, core], target, out_sems.at[q, half, n])

    def done(q):
        for item in group_copies(q):
            item.start()

    blur(
        1,
        mats,
        wide,
        across,
        lambda: copies.wait(0, count),
        lambda: copies.wait(count),
        lambda: None,
        finish,
        done,
    )
    for q in range(4):
        for item in group_copies(q):
            item.wait()


def backward(cover, mats, center, halos, strips):
    half = jax.ShapeDtypeStruct((4,) + PART, F32)
    return pl.pallas_call(
        backward_kernel,
        out_shape=(half, half),
        in_specs=[SMEM] + [VMEM] * 5 + [ANY] * 7,
        out_specs=(ANY, ANY),
        scratch_shapes=[
            pltpu.VMEM(WIDE, F32),
            pltpu.VMEM((2, 4, 768, 128), F32),
            pltpu.VMEM((2, 4, 512, 128), F32),
            pltpu.SemaphoreType.DMA((18,)),
            pltpu.SemaphoreType.DMA((4, 2, 2)),
        ],
        compiler_params=params(16),
        name="backward",
    )(cover, *mats, center, *halos, *strips)


def shares_kernel(mine, got, *outs):
    z, y, x, c = place()
    for k in range(4):
        s = (x + k) % XD

        @pl.loop(0, 4)
        def _(b):
            outs[k][b] = mine[b, s] + got[b, s]


def shares(mine, got):
    part = jax.ShapeDtypeStruct(PART, F32)
    return pl.pallas_call(
        shares_kernel,
        out_shape=(part,) * 4,
        in_specs=[VMEM, VMEM],
        out_specs=(VMEM,) * 4,
        compiler_params=params(8),
        name="shares",
    )(mine, got)


def edges_kernel(*refs):
    pieces, outs = refs[:8], refs[8:12]
    tile, sems, out_sems = refs[12:]
    z, y, x, c = place()
    copies = Copies(sems)
    put_pieces(copies, pieces, lambda h, s: tile.at[:, h, s])
    copies.wait()
    copies = Copies(out_sems)
    for n, (step0, step1) in enumerate(STEPS):
        out1 = outs[n].reshape(*YEDGE) if n < 2 else outs[n]
        copies.add_by_core(c, (edge_of(tile, step0), outs[n]), (edge_of(tile, step1), out1))
    copies.wait()


def edges(pieces):
    return pl.pallas_call(
        edges_kernel,
        out_shape=tuple(jax.ShapeDtypeStruct(s, F32) for s in (ZEDGE, ZEDGE, CORNER, CORNER)),
        in_specs=[ANY] * 8,
        out_specs=(ANY,) * 4,
        scratch_shapes=[
            pltpu.VMEM(TILE, F32),
            pltpu.SemaphoreType.DMA((8,)),
            pltpu.SemaphoreType.DMA((4,)),
        ],
        compiler_params=params(6),
        name="edges",
    )(*pieces)


def slab_kernel(*refs):
    pieces, out = refs[:8], refs[8]
    slab, sems, out_sems = refs[9:]
    z, y, x, c = place()
    copies = Copies(sems)
    put_pieces(copies, pieces, lambda h, s: slab.at[h, s])
    copies.wait()
    copies = Copies(out_sems)
    copies.add(slab, out)
    copies.wait()


def slab(pieces):
    return pl.pallas_call(
        slab_kernel,
        out_shape=jax.ShapeDtypeStruct((2, 4, 2, 128, 256), F32),
        in_specs=[ANY] * 8,
        out_specs=ANY,
        scratch_shapes=[
            pltpu.VMEM((2, 4, 2, 128, 256), F32),
            pltpu.SemaphoreType.DMA((8,)),
            pltpu.SemaphoreType.DMA((1,)),
        ],
        compiler_params=params(6),
        name="slab",
    )(*pieces)


def by_block(pieces, y):
    order = [pieces[0], pieces[3], pieces[2], pieces[1]]
    stack = jnp.stack(order + order[:3])
    return lax.dynamic_slice_in_dim(stack, (YD - y) % YD, 4, axis=0)


def gathered(share):
    return [share] + [x_turn(share, k) for k in (1, 2, 3)]


def local(estimate, views, axial_taps, lateral_taps, cover):
    z, y, x, c = place()

    half = lax.dynamic_slice_in_dim(estimate, 8 * c, 8, axis=0)
    half = jnp.pad(half, ((0, 0), (8, 8), (0, 0))).reshape(4, 2, 18, 8, 256)

    def est_rows(k):
        return lax.dynamic_slice_in_dim(half, 4 * ((y + k) % YD), 6, axis=2)

    def view_rows(k):
        rows = lax.dynamic_slice_in_dim(views[0].reshape(16, 16, 8, 256), 4 * ((y + k) % YD), 4, axis=1)
        return jnp.transpose(rows, (1, 0, 2, 3)).reshape(4, 2, 4, 2, 8, 256)

    parts, views = lax.optimization_barrier(([est_rows(k) for k in range(4)], views))
    pieces = [parts[0]] + [y_turn(parts[k], k) for k in (1, 2, 3)]
    mats = matrices(axial_taps, lateral_taps)
    shown = [view_rows(k) for k in range(4)]
    pieces, mats = lax.optimization_barrier((pieces, mats))
    shown = [shown[0]] + [y_turn(shown[k], k) for k in (1, 2, 3)]
    share = [lax.dynamic_index_in_dim(p, x, 0, keepdims=False)[:, 1:5] for p in pieces]
    share = by_block(share, y)
    for step in range(ITERS):
        if step == 0:
            top = lax.select_n((y + 1) % YD, *pieces)
            bottom = lax.select_n(y, *pieces)
            beside = [blk_shift(top, 1, 0), blk_shift(bottom, -1, 0)]
            tile = pieces + [core_swap(piece) for piece in pieces]
            beside, shown = lax.optimization_barrier((beside, shown))
            tile += beside + [core_swap(part) for part in beside]
        else:
            pieces = gathered(share)
            pieces = pieces + [core_swap(piece) for piece in pieces]
            rims = [core_step(e, steps) for e, steps in zip(edges(pieces), STEPS)]
            swapped = core_swap(jnp.concatenate([rim.reshape(-1, 8, 256) for rim in rims]))
            tile = pieces + rims + [swapped]
        center, rims = forward(step == 0, mats, tile, shown)
        halos = [blk_shift(e, *d) for e, d in zip(rims, FACES)]
        low, high = halos[0], halos[1]
        strips = [blk_shift(jnp.stack([low[r], high[r]]), 0, dy) for r, dy in ((3, 1), (0, -1))]
        mine, other = backward(cover, mats, center, halos, strips)
        terms = shares(mine, core_swap(other))
        total = terms[0]
        for k in (1, 2, 3):
            total = total + x_turn(terms[k], k)
        share = share * jnp.exp(total)
    share = share.reshape(4, 2, 32, 256)
    parts = [lax.dynamic_index_in_dim(share, (y + k) % YD, 0, keepdims=False) for k in range(4)]
    parts = [parts[0]] + [y_turn(parts[k], k) for k in (1, 2, 3)]
    strip = by_block(parts, y)
    strip = jnp.transpose(strip, (1, 0, 2, 3)).reshape(2, 128, 256)
    pieces = gathered(strip)
    pieces = pieces + [core_swap(piece) for piece in pieces]
    return slab(pieces).reshape(16, 128, 256)


def solution(mesh):
    in_specs = (
        P("blk", None, None),
        P("view", "blk", None, None),
        P("view", None),
        P("view", None, None),
        P("view", None),
    )
    out_specs = P("blk", None, None)
    return jax.shard_map(local, mesh=mesh, in_specs=in_specs, out_specs=out_specs, check_vma=False)
```
